32 devices in a mesh: row: 4 (over z), col: 4 (over y, core), occ: 2 (over x).
Axes of the slice: x: 2, y: 2, z: 4, core: 2. Of those that a mesh axis runs over, the one named last changes fastest.
Arguments:
- amplitudes: bfloat16 [2, 2048, 8192], P(None, ('row', 'occ'), 'col'), may hold values from -6 to 6
- integrals: bfloat16 [2, 8192, 8192], P(None, 'row', 'col'), may hold values from -0.09375 to 0.09375
- virtual_energy: float32 [256], replicated, may hold values from 0.4 to 3
- occupied_energy: float32 [128], replicated, may hold values from -2 to -0.4
- virtual_count: int32 [8], replicated, may hold values from 16 to 32, as said below
- occupied_count: int32 [8], replicated, may hold values from 8 to 16, as said below
Outputs:
- update: float32 [2, 2048, 8192], P(None, ('col', 'occ'), 'row')
The draws below stay inside these ranges and needn't reach their ends.
Inputs may be any that keep to these rules, and one draw needn't show every extreme that they name: `virtual_count`: orbitals in each irrep block; some irrep fills all 32 slots. `occupied_count`: orbitals in each irrep block; some irrep fills all 16 slots.
All inputs are finite; a program needn't handle non-finite values.
Results may differ from the reference program's by a relative error of at most 0.0003.
Values may be sent and summed in bfloat16 or wider, within the bound.
No kernel may reach another device: no remote copies, remote signals or barrier semaphores. Data moves between devices by JAX's collectives and lax.ppermute only.
A program may use at most 128 MiB of HBM per device.

```python
import math
import jax
import jax.numpy as jnp
from jax import lax

VCAP = 32
OCAP = 16
NSYM = 2
WV = 256
WO = 128
VPAIRS = 8192
OPAIRS = 2048
TILE = 2048


def draw_virtual_count(key, part):
    first_key = jax.random.fold_in(key, 11)
    second_key = jax.random.fold_in(key, 12)
    counts = jax.random.randint(first_key, (8,), VCAP // 2, VCAP + 1, dtype=jnp.int32)
    fullest = jax.random.randint(second_key, (), 0, 8, dtype=jnp.int32)
    return jnp.where(jnp.arange(8, dtype=jnp.int32) == fullest, VCAP, counts).astype(jnp.int32)


def draw_occupied_count(key, part):
    first_key = jax.random.fold_in(key, 21)
    second_key = jax.random.fold_in(key, 22)
    counts = jax.random.randint(first_key, (8,), OCAP // 2, OCAP + 1, dtype=jnp.int32)
    fullest = jax.random.randint(second_key, (), 0, 8, dtype=jnp.int32)
    return jnp.where(jnp.arange(8, dtype=jnp.int32) == fullest, OCAP, counts).astype(jnp.int32)


def with_spikes(values, key, source, target, parts, factor):
    owner, partner = [(jnp.arange(values.shape[position]) // (values.shape[position] // parts)).reshape([-1 if axis == position else 1 for axis in range(values.ndim)]) for position in (source, target)]
    chosen = jax.random.permutation(key, parts)[partner]
    strong = (owner == chosen) | (owner == (partner + parts // 2) % parts)
    return jnp.where(strong, factor * values, values)


def level_of(stream_key, extent, pieces, least, largest):
    level, own = 1.0, jax.random.fold_in(stream_key, 6)
    for axis_at, blocks in pieces:
        heights = jnp.exp(jax.random.uniform(jax.random.fold_in(own, axis_at), (blocks,), jnp.float32, least / len(pieces), largest / len(pieces)))
        level = level * jnp.repeat(heights, extent[axis_at] // blocks).reshape([-1 if axis == axis_at else 1 for axis in range(len(extent))])
    return level


def gaussian(stream_key, dims, width, limit, pieces=(), kind=jnp.bfloat16):
    array = width * jax.random.normal(stream_key, dims, jnp.float32)
    if pieces:
        array = array * level_of(stream_key, dims, pieces, -0.22, 0.18)
    return jnp.clip(array, -limit, limit).astype(kind)


def bell_draw_with(stream_key, shape, scale, most, pieces, heavy, held_as=jnp.bfloat16):
    drawn = scale * jax.random.normal(stream_key, shape, jnp.float32)
    if pieces:
        drawn = drawn * level_of(stream_key, shape, pieces, -0.22, 0.18)
    return jnp.clip(with_spikes(drawn, jax.random.fold_in(stream_key, 3), *heavy), -most, most).astype(held_as)


def setup_inputs(seed: int = 0) -> dict:
    keys = jax.random.split(jax.random.key(seed), 7)
    return {
        "amplitudes": bell_draw_with(keys[0], (NSYM, OPAIRS, VPAIRS), 1.0, 6.0, ((1, 8), (2, 4)), (2, 1, 8, 2.0)),
        "integrals": gaussian(keys[1], (NSYM, VPAIRS, VPAIRS), (VPAIRS // 2) ** -0.5, 0.09375, ((1, 4), (2, 4))),
        "virtual_energy": jnp.clip(jnp.exp(jax.random.uniform(keys[2], (WV,), jnp.float32, math.log(0.4), math.log(3.0))), 0.4, 3.0),
        "occupied_energy": jnp.clip(jax.random.uniform(keys[3], (WO,), jnp.float32, -2.0, -0.4), -2.0, -0.4),
        "virtual_count": draw_virtual_count(jax.random.fold_in(keys[6], 71), 0),
        "occupied_count": draw_occupied_count(jax.random.fold_in(keys[6], 71), 0),
    }


def virtual_maps():
    slot = jnp.arange(VPAIRS, dtype=jnp.int32)
    symmetry = jnp.arange(NSYM, dtype=jnp.int32)[:, None]
    offset = slot // WV
    first_orb = jnp.broadcast_to(slot % WV, (NSYM, VPAIRS))
    second_orb = jnp.bitwise_xor(first_orb, symmetry * VCAP + offset[None, :])
    mate = offset[None, :] * WV + second_orb
    return first_orb, second_orb, mate


def occupied_maps():
    slot = jnp.arange(OPAIRS, dtype=jnp.int32)
    symmetry = jnp.arange(NSYM, dtype=jnp.int32)[:, None]
    offset = slot // WO
    first_orb = jnp.broadcast_to(slot % WO, (NSYM, OPAIRS))
    second_orb = jnp.bitwise_xor(first_orb, symmetry * OCAP + offset[None, :])
    mate = offset[None, :] * WO + second_orb
    return first_orb, second_orb, mate


def reference(amplitudes, integrals, virtual_energy, occupied_energy, virtual_count, occupied_count):
    first_virtual, second_virtual, virtual_mate = virtual_maps()
    first_occupied, second_occupied, occupied_mate = occupied_maps()
    virtual_ok = (first_virtual % VCAP < virtual_count[first_virtual // VCAP]) & (second_virtual % VCAP < virtual_count[second_virtual // VCAP])
    occupied_ok = (first_occupied % OCAP < occupied_count[first_occupied // OCAP]) & (second_occupied % OCAP < occupied_count[second_occupied // OCAP])
    pair_energy = virtual_energy[first_virtual] + virtual_energy[second_virtual]
    hole_energy = occupied_energy[first_occupied] + occupied_energy[second_occupied]
    results = []
    for symmetry in range(NSYM):
        allowed = occupied_ok[symmetry][:, None] & virtual_ok[symmetry][None, :]
        masked = jnp.where(allowed, amplitudes[symmetry], jnp.zeros((), amplitudes.dtype))
        coupling = integrals[symmetry]

        def add_group(accumulated, group):
            start_col = (group * TILE).astype(jnp.int32)
            amp_part = lax.dynamic_slice_in_dim(masked, start_col, TILE, 1)
            int_part = lax.dynamic_slice_in_dim(coupling, start_col, TILE, 1)
            product = lax.dot_general(amp_part, int_part, (((1,), (1,)), ((), ())), preferred_element_type=jnp.float32)
            return accumulated + product, None

        ladder, _ = lax.scan(add_group, jnp.zeros((OPAIRS, VPAIRS), jnp.float32), jnp.arange(VPAIRS // TILE, dtype=jnp.int32))
        mirrored = jnp.take(jnp.take(ladder, occupied_mate[symmetry], axis=0), virtual_mate[symmetry], axis=1)
        symmetrized = ladder + mirrored
        denominator = pair_energy[symmetry][None, :] - hole_energy[symmetry][:, None]
        results.append(jnp.where(allowed, symmetrized / denominator, jnp.zeros((), jnp.float32)))
    return jnp.stack(results, axis=0)
```

```python
import functools
import jax
import jax.numpy as jnp
from jax import lax
from jax.experimental import pallas as pl
from jax.experimental.pallas import tpu as pltpu
from jax.sharding import PartitionSpec as P

F32, BF16, I32, I16 = jnp.float32, jnp.bfloat16, jnp.int32, jnp.int16
LANES = 128
TILE_ROWS = 16
ANY = pl.BlockSpec(memory_space=pl.ANY)


def table_value(values_table, positions):
    places = jnp.arange(values_table.shape[0], dtype=jnp.int32)
    matches = positions[..., None] == places
    return jnp.sum(jnp.where(matches, values_table, jnp.zeros((), values_table.dtype)), axis=-1)


def is_orbital(counts, orbital, capacity):
    return orbital % capacity < table_value(counts, orbital // capacity)


def pair_orbitals(slot, group_width, capacity, sym_count):
    symmetry = jnp.arange(sym_count, dtype=jnp.int32)[:, None]
    offset = slot // group_width
    first_orb = jnp.broadcast_to(slot % group_width, (sym_count, slot.shape[0]))
    second_orb = jnp.bitwise_xor(first_orb, symmetry * capacity + offset[None, :])
    mate = offset[None, :] * group_width + second_orb
    return (first_orb, second_orb, mate)


def mirror_block(block, row_index, col_index):
    return jnp.take(jnp.take(block, row_index, axis=0), col_index, axis=1)


def on_device_general(
    amplitudes, integrals, virtual_energy, occupied_energy, virtual_count, occupied_count
):
    row_number = lax.axis_index("row")
    col_number = lax.axis_index("col")
    occ_number = lax.axis_index("occ")
    sym_count = amplitudes.shape[0]
    share_rows = amplitudes.shape[1]
    tile_width = amplitudes.shape[2]
    virt_slots = virtual_energy.shape[0]
    occ_slots = occupied_energy.shape[0]
    virt_cap = virt_slots // 8
    occ_cap = occ_slots // 8
    gathered = lax.all_gather(amplitudes, "row", axis=1, tiled=True)
    gathered_row = jnp.arange(gathered.shape[1], dtype=jnp.int32)
    source_slot = (
        2 * (gathered_row // share_rows) + occ_number
    ) * share_rows + gathered_row % share_rows
    first_source, second_source, _ = pair_orbitals(source_slot, occ_slots, occ_cap, sym_count)
    source_ok = is_orbital(occupied_count, first_source, occ_cap) & is_orbital(
        occupied_count, second_source, occ_cap
    )
    contract_slot = col_number * tile_width + jnp.arange(tile_width, dtype=jnp.int32)
    first_contract, second_contract, _ = pair_orbitals(
        contract_slot, virt_slots, virt_cap, sym_count
    )
    contract_ok = is_orbital(virtual_count, first_contract, virt_cap) & is_orbital(
        virtual_count, second_contract, virt_cap
    )
    masked = jnp.where(
        source_ok[:, :, None] & contract_ok[:, None, :], gathered, jnp.zeros((), gathered.dtype)
    )
    summed = lax.psum_scatter(
        jnp.einsum("sqd,spd->qsp", masked, integrals, preferred_element_type=jnp.float32),
        "col",
        scatter_dimension=0,
        tiled=True,
    )
    ladder = summed.transpose(1, 0, 2)
    row_base = (2 * col_number + occ_number) * share_rows
    output_slot = row_base + jnp.arange(share_rows, dtype=jnp.int32)
    first_occupied, second_occupied, occupied_mate = pair_orbitals(
        output_slot, occ_slots, occ_cap, sym_count
    )
    col_base = row_number * tile_width
    output_pair = col_base + jnp.arange(tile_width, dtype=jnp.int32)
    first_virtual, second_virtual, virtual_mate = pair_orbitals(
        output_pair, virt_slots, virt_cap, sym_count
    )
    mirrored = jax.vmap(mirror_block)(ladder, occupied_mate - row_base, virtual_mate - col_base)
    symmetrized = ladder + mirrored
    hole_ok = is_orbital(occupied_count, first_occupied, occ_cap) & is_orbital(
        occupied_count, second_occupied, occ_cap
    )
    pair_ok = is_orbital(virtual_count, first_virtual, virt_cap) & is_orbital(
        virtual_count, second_virtual, virt_cap
    )
    pair_energy = table_value(virtual_energy, first_virtual) + table_value(
        virtual_energy, second_virtual
    )
    hole_energy = table_value(occupied_energy, first_occupied) + table_value(
        occupied_energy, second_occupied
    )
    denominator = pair_energy[:, None, :] - hole_energy[:, :, None]
    allowed = hole_ok[:, :, None] & pair_ok[:, None, :]
    return jnp.where(allowed, symmetrized / denominator, jnp.zeros((), jnp.float32))


class Plan:
    def __init__(self, amp_shape, int_shape, rows, virt_slots, occ_slots):
        self.syms, self.share, self.width = amp_shape
        self.pairs = int_shape[1]
        self.rows = rows
        self.virt_slots, self.occ_slots = virt_slots, occ_slots
        self.virt_cap, self.occ_cap = virt_slots // 8, occ_slots // 8
        self.tiles = self.width // LANES
        self.row_tiles = self.share // TILE_ROWS
        self.pay_tiles = self.syms * self.tiles * self.row_tiles
        half = self.share // 2
        self.rep_rows = [half + self.occ_slots // 2] + [half] * (self.syms - 1)
        self.enc_tiles = sum(self.rep_rows) // TILE_ROWS
        self.at_ndt = 2
        self.at_first = self.at_ndt + self.syms
        self.at_reps = self.at_first + self.syms * self.tiles
        self.at_self = self.at_reps + self.syms * rows


def scalars(plan, tab, sym, share):
    reps = tab[plan.at_reps + sym * plan.rows + share]
    selfs = tab[plan.at_self + sym * plan.rows + share]
    return reps, selfs, tab[plan.at_ndt + sym]


def band(rel_row):
    return (lax.broadcasted_iota(I32, (2 * LANES, LANES), 0) == rel_row).astype(BF16)


def pack_kernel(plan, tab, amp, dest, rel, pay, acc):
    pay[...] = jnp.zeros_like(pay)
    row = tab[0]
    base = jnp.int32(0)
    for sym in range(plan.syms):
        reps, selfs, ndt = scalars(plan, tab, sym, row)
        nrt = 2 * reps + selfs
        pick = (
            lax.broadcasted_iota(I32, (plan.share, plan.share), 0) == dest[sym : sym + 1, :]
        ).astype(BF16)
        compact = jnp.dot(pick, amp[sym], preferred_element_type=F32).astype(BF16)
        acc[...] = jnp.zeros_like(acc)
        for tile in range(plan.tiles):
            at = sym * plan.tiles + tile
            placed = lax.dot_general(
                compact[:, tile * LANES : (tile + 1) * LANES],
                band(rel[at : at + 1, :]),
                (((1,), (1,)), ((), ())),
                preferred_element_type=F32,
            )
            first = tab[plan.at_first + at]
            acc[first] += placed[:, :LANES]
            acc[first + 1] += placed[:, LANES:]

        def put(tile, _, base=base, nrt=nrt):
            start = pl.multiple_of((base + tile * nrt) * TILE_ROWS, TILE_ROWS)
            pay[pl.ds(start, plan.share), :] = acc[tile].astype(BF16)
            return 0

        lax.fori_loop(0, ndt, put, 0)
        base = base + nrt * ndt


def pack(plan, tab, amp, dest, rel):
    pay_rows = plan.pay_tiles * TILE_ROWS + plan.share
    vm = pl.BlockSpec(memory_space=pltpu.VMEM)
    return pl.pallas_call(
        functools.partial(pack_kernel, plan),
        out_shape=jax.ShapeDtypeStruct((pay_rows, LANES), BF16),
        in_specs=[pl.BlockSpec(memory_space=pltpu.SMEM), vm, vm, vm],
        out_specs=vm,
        scratch_shapes=[pltpu.VMEM((plan.tiles + 1, plan.share, LANES), F32)],
        compiler_params=pltpu.CompilerParams(vmem_limit_bytes=40 << 20),
        name="pack",
    )(tab, amp, dest, rel)


def share_of(plan, row, kind):
    step, side = kind
    if step == 0:
        return row, row >= 0
    if side == "right":
        return row - step, row >= step
    if side == "left":
        return row + step, row + step < plan.rows
    share = jnp.where(row >= plan.rows // 2, row - step, row + step)
    return share, (share >= 0) & (share < plan.rows)


def lane_mates(plan, rows, sym, fbase, tile):
    flip = sym * plan.virt_cap + fbase + (tile * LANES) // plan.virt_slots
    return lax.broadcasted_iota(I32, (rows, LANES), 1) ^ flip


def lane_take(x, index):
    return jnp.take_along_axis(x, index, axis=1)


def ladder_kernel(plan, kind, pay_rows, enc_rows, ptile, tab, rel, *refs):
    pays, (ints, out, pay, dense, prod, enc, sem) = refs[:-7], refs[-7:]
    sym, pt = pl.program_id(0), pl.program_id(1)
    steps = plan.pairs // ptile
    row = tab[0]
    share, active = share_of(plan, row, kind)

    @pl.when(active & (sym == 0) & (pt == 0))
    def _():
        if len(pays) == 1:
            copy = pltpu.make_async_copy(pays[0], pay.at[pl.ds(0, pay_rows)], sem)
            copy.start()
            copy.wait()
        else:
            upper = row >= plan.rows // 2

            @pl.when(upper)
            def _():
                copy = pltpu.make_async_copy(pays[0], pay.at[pl.ds(0, pay_rows)], sem)
                copy.start()
                copy.wait()

            @pl.when(jnp.logical_not(upper))
            def _():
                copy = pltpu.make_async_copy(pays[1], pay.at[pl.ds(0, pay_rows)], sem)
                copy.start()
                copy.wait()

    @pl.when(active)
    def _():
        reps, selfs, ndt = scalars(plan, tab, sym, share)
        nrt = 2 * reps + selfs

        @pl.when(pt == 0)
        def _():
            reps0, selfs0, ndt0 = scalars(plan, tab, 0, share)
            base = jnp.where(sym == 0, 0, (2 * reps0 + selfs0) * ndt0)
            for tile in range(plan.tiles):
                at = sym * plan.tiles + tile
                first = tab[plan.at_first + at]
                parts = []
                for step in range(2):
                    use = jnp.maximum(jnp.minimum(first + step, ndt - 1), 0)
                    start = pl.multiple_of((base + use * nrt) * TILE_ROWS, TILE_ROWS)
                    parts.append(pay[pl.ds(start, plan.share), :])
                dense[:, tile * LANES : (tile + 1) * LANES] = jnp.dot(
                    jnp.concatenate(parts, axis=1),
                    band(rel[pl.ds(at, 1), :]),
                    preferred_element_type=F32,
                ).astype(BF16)

        product = lax.dot_general(
            dense[...], ints[0], (((1,), (1,)), ((), ())), preferred_element_type=F32
        )
        prod[:, pl.ds(pl.multiple_of(pt * ptile, ptile), ptile)] = product

        @pl.when(pt == steps - 1)
        def _():
            reps0, selfs0, _ = scalars(plan, tab, 0, share)
            enc_base = jnp.where(sym == 0, 0, reps0 + selfs0)
            fbase = row * (plan.pairs // plan.virt_slots)

            def chunk(k, _):
                mate_row = pl.multiple_of((k + reps) * TILE_ROWS, TILE_ROWS)
                own_row = pl.multiple_of(
                    jnp.where(k < reps, k, k + reps) * TILE_ROWS, TILE_ROWS
                )
                to_row = pl.multiple_of((enc_base + k) * TILE_ROWS, TILE_ROWS)
                sums, top = [], None
                for v in range(plan.pairs // LANES):
                    lanes = slice(v * LANES, (v + 1) * LANES)
                    mirrored = lane_take(
                        prod[pl.ds(mate_row, TILE_ROWS), lanes],
                        lane_mates(plan, TILE_ROWS, sym, fbase, v),
                    )
                    both = prod[pl.ds(own_row, TILE_ROWS), lanes] + mirrored
                    sums.append(both)
                    top = jnp.abs(both) if top is None else jnp.maximum(top, jnp.abs(both))
                peak = jnp.maximum(jnp.max(top, axis=1, keepdims=True), 1e-30)
                power = jnp.floor(jnp.log2(32000.0 / peak))
                scale = jnp.exp2(power)
                for v, both in enumerate(sums):
                    enc[pl.ds(to_row, TILE_ROWS), v * LANES : (v + 1) * LANES] = (
                        jnp.round(both * scale).astype(I32).astype(I16)
                    )
                enc[pl.ds(to_row, TILE_ROWS), plan.pairs :] = (
                    jnp.broadcast_to(power, (TILE_ROWS, LANES)).astype(I32).astype(I16)
                )
                return 0

            lax.fori_loop(0, reps + selfs, chunk, 0)

    @pl.when(active & (sym == plan.syms - 1) & (pt == steps - 1))
    def _():
        copy = pltpu.make_async_copy(enc.at[pl.ds(0, enc_rows)], out, sem)
        copy.start()
        copy.wait()


def ladder_call(plan, kind, tab, rel, pays, integrals, enc_rows):
    ptile = min(512, plan.pairs)
    pay_rows = pays[0].shape[0]

    def int_block(sym, pt, tab):
        _, active = share_of(plan, tab[0], kind)
        use = active.astype(I32)
        return (sym * use, pt * use, 0)

    grid_spec = pltpu.PrefetchScalarGridSpec(
        num_scalar_prefetch=1,
        grid=(plan.syms, plan.pairs // ptile),
        in_specs=[pl.BlockSpec(rel.shape, lambda sym, pt, tab: (0, 0))]
        + [ANY] * len(pays)
        + [pl.BlockSpec((1, ptile, plan.width), int_block)],
        out_specs=ANY,
        scratch_shapes=[
            pltpu.VMEM((plan.pay_tiles * TILE_ROWS + plan.share, LANES), BF16),
            pltpu.VMEM((plan.share, plan.width), BF16),
            pltpu.VMEM((plan.share, plan.pairs), F32),
            pltpu.VMEM((plan.enc_tiles * TILE_ROWS, plan.pairs + LANES), I16),
            pltpu.SemaphoreType.DMA,
        ],
    )
    return pl.pallas_call(
        functools.partial(ladder_kernel, plan, kind, pay_rows, enc_rows, ptile),
        out_shape=jax.ShapeDtypeStruct((enc_rows, plan.pairs + LANES), I16),
        grid_spec=grid_spec,
        compiler_params=pltpu.CompilerParams(
            dimension_semantics=("arbitrary", "arbitrary"), vmem_limit_bytes=48 << 20
        ),
        cost_estimate=pl.CostEstimate(
            flops=2 * plan.syms * plan.share * plan.width * plan.pairs,
            bytes_accessed=2 * plan.syms * plan.width * plan.pairs,
            transcendentals=0,
        ),
        name="ladder",
    )(tab, rel, *pays, integrals)


def finish_kernel(plan, enc_rows, wtile, tab, line, hole, pair, pair_ok, *refs):
    sources, (out, held, sems) = refs[:-3], refs[-3:]
    step = pl.program_id(0)
    row, col = tab[0], tab[1]
    away = jnp.abs(row - col)
    which = jnp.where(away == 0, 0, jnp.where(away == 1, jnp.where(col < row, 1, 2), away + 1))

    @pl.when(step == 0)
    def _():
        for number in range(len(sources) // 4):

            @pl.when(which == number)
            def _():
                copies = [
                    pltpu.make_async_copy(
                        sources[4 * number + part],
                        held.at[part, pl.ds(0, enc_rows)],
                        sems.at[part],
                    )
                    for part in range(4)
                ]
                for copy in copies:
                    copy.start()
                for copy in copies:
                    copy.wait()

    fbase = row * (plan.pairs // plan.virt_slots) + step * (wtile // plan.virt_slots)
    enc_base = jnp.int32(0)
    for sym in range(plan.syms):
        reps, selfs, _ = scalars(plan, tab, sym, col)
        count = plan.rep_rows[sym]
        rows = pl.ds(pl.multiple_of(enc_base * TILE_ROWS, TILE_ROWS), count)
        enc_base = enc_base + reps + selfs
        live = lax.broadcasted_iota(I32, (count, LANES), 0) < (reps + selfs) * TILE_ROWS
        scales = [
            jnp.exp2(-held[part, rows, pl.ds(plan.pairs, LANES)].astype(I32).astype(F32))
            for part in range(4)
        ]
        own, mates = [], []
        for v in range(wtile // LANES):
            lanes = pl.ds(pl.multiple_of(step * wtile + v * LANES, LANES), LANES)
            total = None
            for part in range(4):
                term = held[part, rows, lanes].astype(I32).astype(F32) * scales[part]
                total = term if total is None else total + term
            total = jnp.where(live, total, 0.0)
            own.append(total)
            mates.append(lane_take(total, lane_mates(plan, count, sym, fbase, v)))
        both = jnp.concatenate(
            [jnp.concatenate(own, axis=1), jnp.concatenate(mates, axis=1)], axis=0
        )
        pick = (
            lax.broadcasted_iota(I32, (plan.share, 2 * count), 1) == line[sym]
        ).astype(BF16)
        result = None
        rest = both
        for _ in range(3):
            term = rest.astype(BF16)
            rest = rest - term.astype(F32)
            part = jnp.dot(pick, term, preferred_element_type=F32)
            result = part if result is None else result + part
        allowed = (line[sym] >= 0) & (pair_ok[sym] > 0)
        out[sym] = jnp.where(allowed, result / (pair[sym] - hole[sym]), 0.0)


def finish(plan, tab, line, hole, pair, pair_ok, sources):
    enc_rows = sources[0].shape[0]
    wtile = min(256, plan.pairs)
    whole = lambda shape: pl.BlockSpec(shape, lambda i, tab: (0,) * len(shape))
    tiled = pl.BlockSpec((plan.syms, 1, wtile), lambda i, tab: (0, 0, i))
    grid_spec = pltpu.PrefetchScalarGridSpec(
        num_scalar_prefetch=1,
        grid=(plan.pairs // wtile,),
        in_specs=[whole(line.shape), whole(hole.shape), tiled, tiled] + [ANY] * len(sources),
        out_specs=pl.BlockSpec((plan.syms, plan.share, wtile), lambda i, tab: (0, 0, i)),
        scratch_shapes=[
            pltpu.VMEM((4, plan.enc_tiles * TILE_ROWS, plan.pairs + LANES), I16),
            pltpu.SemaphoreType.DMA((4,)),
        ],
    )
    return pl.pallas_call(
        functools.partial(finish_kernel, plan, enc_rows, wtile),
        out_shape=jax.ShapeDtypeStruct((plan.syms, plan.share, plan.pairs), F32),
        grid_spec=grid_spec,
        compiler_params=pltpu.CompilerParams(
            dimension_semantics=("arbitrary",), vmem_limit_bytes=48 << 20
        ),
        name="finish",
    )(tab, line, hole, pair, pair_ok, *sources)


def occupied_share(plan, counts, share_number):
    slot = share_number * plan.share + jnp.arange(plan.share, dtype=I32)
    first, second, mate = pair_orbitals(slot, plan.occ_slots, plan.occ_cap, plan.syms)
    ok = is_orbital(counts, first, plan.occ_cap) & is_orbital(counts, second, plan.occ_cap)
    lead = jnp.minimum(slot[None, :], mate)
    is_rep = ok & (first < second)
    is_self = ok & (first == second)
    before = slot[None, None, :] < lead[:, :, None]
    rank = jnp.sum((is_rep[:, None, :] & before).astype(I32), axis=-1)
    self_rank = jnp.sum((is_self[:, None, :] & before).astype(I32), axis=-1)
    return first, second, ok, is_rep, is_self, rank, self_rank


def padded(count):
    return (count + TILE_ROWS - 1) // TILE_ROWS


def line_tables(plan, virtual_energy, occupied_energy, virtual_count, occupied_count):
    row = lax.axis_index("row")
    col = lax.axis_index("col")
    occ = lax.axis_index("occ")
    syms = plan.syms
    slots = jnp.arange(2 * plan.rows * plan.share, dtype=I32)
    first, second, _ = pair_orbitals(slots, plan.occ_slots, plan.occ_cap, syms)
    ok = is_orbital(occupied_count, first, plan.occ_cap) & is_orbital(
        occupied_count, second, plan.occ_cap
    )
    grouped = lambda x: jnp.sum(x.astype(I32).reshape(syms, plan.rows, 2, plan.share), axis=-1)
    reps_all = padded(grouped(ok & (first < second)))
    selfs_all = padded(grouped(ok & (first == second)))
    reps = jnp.where(occ == 0, reps_all[:, :, 0], reps_all[:, :, 1])
    selfs = jnp.where(occ == 0, selfs_all[:, :, 0], selfs_all[:, :, 1])
    slot = col * plan.width + jnp.arange(plan.width, dtype=I32)
    first, second, _ = pair_orbitals(slot, plan.virt_slots, plan.virt_cap, syms)
    ok = is_orbital(virtual_count, first, plan.virt_cap) & is_orbital(
        virtual_count, second, plan.virt_cap
    )
    ok = ok.reshape(syms, plan.tiles, LANES)
    per_tile = jnp.sum(ok.astype(I32), axis=-1)
    tile_ids = jnp.arange(plan.tiles, dtype=I32)
    starts = jnp.sum(
        jnp.where(tile_ids[None, None, :] < tile_ids[None, :, None], per_tile[:, None, :], 0), axis=-1
    )
    lane_ids = jnp.arange(LANES, dtype=I32)
    within = jnp.sum(
        (ok[:, :, None, :] & (lane_ids[None, :] < lane_ids[:, None])).astype(I32), axis=-1
    )
    firsts = starts // LANES
    rel = jnp.where(ok, within + (starts % LANES)[:, :, None], -1)
    ndt = (jnp.sum(per_tile, axis=-1) + LANES - 1) // LANES
    tab = jnp.concatenate(
        [jnp.stack([row, col]).astype(I32), ndt, firsts.reshape(-1), reps.reshape(-1), selfs.reshape(-1)]
    )
    _, _, ok, is_rep, is_self, rank, self_rank = occupied_share(
        plan, occupied_count, 2 * row + occ
    )
    n_rep = padded(jnp.sum(is_rep.astype(I32), axis=-1, keepdims=True)) * TILE_ROWS
    dest = jnp.where(is_self, 2 * n_rep + self_rank, jnp.where(is_rep, rank, n_rep + rank))
    dest = jnp.where(ok, dest, -1)
    first, second, ok, is_rep, is_self, rank, self_rank = occupied_share(
        plan, occupied_count, 2 * col + occ
    )
    n_rep = padded(jnp.sum(is_rep.astype(I32), axis=-1, keepdims=True)) * TILE_ROWS
    count = jnp.array(plan.rep_rows, I32)[:, None]
    line = jnp.where(is_self, n_rep + self_rank, jnp.where(is_rep, rank, count + rank))
    line = jnp.where(ok, line, -1)
    hole = table_value(occupied_energy, first) + table_value(occupied_energy, second)
    slot = row * plan.pairs + jnp.arange(plan.pairs, dtype=I32)
    first, second, _ = pair_orbitals(slot, plan.virt_slots, plan.virt_cap, syms)
    pair_ok = is_orbital(virtual_count, first, plan.virt_cap) & is_orbital(
        virtual_count, second, plan.virt_cap
    )
    pair = table_value(virtual_energy, first) + table_value(virtual_energy, second)
    return (
        tab,
        dest,
        rel.reshape(syms * plan.tiles, LANES),
        line[:, :, None],
        hole[:, :, None],
        pair[:, None, :],
        pair_ok.astype(I32)[:, None, :],
    )


def send_to_roots(plan, enc, kind):
    received = []
    for flip in range(1, plan.rows):
        pairs = []
        for row in range(plan.rows):
            step, side = kind
            if side == "right":
                root = row - step
            elif side == "left":
                root = row + step
            else:
                root = row - step if row >= plan.rows // 2 else row + step
            if 0 <= root < plan.rows:
                pairs.append((row * plan.rows + (root ^ flip), row * plan.rows + root))
        received.append(lax.ppermute(enc, ("row", "col"), pairs))
    return received


def line_body(plan, pay_tiles, enc_tiles, tables, packed, integrals):
    tab, rel, line, hole, pair, pair_ok = tables
    enc_rows = enc_tiles * TILE_ROWS
    pay = packed[: pay_tiles * TILE_ROWS]
    n = plan.rows
    sources = []

    def work(kind, pays):
        enc = ladder_call(plan, kind, tab, rel, pays, integrals, enc_rows)
        sources.extend([enc] + send_to_roots(plan, enc, kind))

    rights, lefts = [pay], [pay]
    for step in range(1, n):
        rights.append(
            lax.ppermute(rights[-1], "row", [(i, i + 1) for i in range(step - 1, n - 1)])
        )
        lefts.append(
            lax.ppermute(lefts[-1], "row", [(i + 1, i) for i in range(0, n - step)])
        )
    work((0, ""), [pay])
    work((1, "right"), [rights[1]])
    work((1, "left"), [lefts[1]])
    for step in range(2, n):
        work((step, ""), [rights[step], lefts[step]])
    return finish(plan, tab, line, hole, pair, pair_ok, sources)


def on_device_line(
    rows, amplitudes, integrals, virtual_energy, occupied_energy, virtual_count, occupied_count
):
    plan = Plan(
        amplitudes.shape, integrals.shape, rows, virtual_energy.shape[0], occupied_energy.shape[0]
    )
    tab, dest, rel, *rest = line_tables(
        plan, virtual_energy, occupied_energy, virtual_count, occupied_count
    )
    packed = pack(plan, tab, amplitudes, dest, rel)
    return line_body(
        plan, plan.pay_tiles, plan.enc_tiles, (tab, rel, *rest), packed, integrals
    )


def solution(mesh):
    rows, cols = mesh.shape["row"], mesh.shape["col"]
    placed = (P(None, ("row", "occ"), "col"), P(None, "row", "col"), P(), P(), P(), P())
    on_device = on_device_general
    if rows == 4 and cols == 4:
        on_device = functools.partial(on_device_line, rows)
    return jax.shard_map(
        on_device,
        mesh=mesh,
        in_specs=placed,
        out_specs=P(None, ("col", "occ"), "row"),
        check_vma=False,
    )
```

```python
import functools
import jax
import jax.numpy as jnp
from jax import lax
from jax.experimental import pallas as pl
from jax.experimental.pallas import tpu as pltpu
from jax.sharding import PartitionSpec as P

F32, BF16, I32, I16 = jnp.float32, jnp.bfloat16, jnp.int32, jnp.int16
LANES = 128
TILE_ROWS = 16
ANY = pl.BlockSpec(memory_space=pltpu.HBM)


def table_value(values_table, positions):
    places = jnp.arange(values_table.shape[0], dtype=jnp.int32)
    matches = positions[..., None] == places
    return jnp.sum(jnp.where(matches, values_table, jnp.zeros((), values_table.dtype)), axis=-1)


def is_orbital(counts, orbital, capacity):
    return orbital % capacity < table_value(counts, orbital // capacity)


def pair_orbitals(slot, group_width, capacity, sym_count):
    symmetry = jnp.arange(sym_count, dtype=jnp.int32)[:, None]
    offset = slot // group_width
    first_orb = jnp.broadcast_to(slot % group_width, (sym_count, slot.shape[0]))
    second_orb = jnp.bitwise_xor(first_orb, symmetry * capacity + offset[None, :])
    mate = offset[None, :] * group_width + second_orb
    return (first_orb, second_orb, mate)


def mirror_block(block, row_index, col_index):
    return jnp.take(jnp.take(block, row_index, axis=0), col_index, axis=1)


def on_device_general(
    amplitudes, integrals, virtual_energy, occupied_energy, virtual_count, occupied_count
):
    row_number = lax.axis_index("row")
    col_number = lax.axis_index("col")
    occ_number = lax.axis_index("occ")
    sym_count = amplitudes.shape[0]
    share_rows = amplitudes.shape[1]
    tile_width = amplitudes.shape[2]
    virt_slots = virtual_energy.shape[0]
    occ_slots = occupied_energy.shape[0]
    virt_cap = virt_slots // 8
    occ_cap = occ_slots // 8
    gathered = lax.all_gather(amplitudes, "row", axis=1, tiled=True)
    gathered_row = jnp.arange(gathered.shape[1], dtype=jnp.int32)
    source_slot = (
        2 * (gathered_row // share_rows) + occ_number
    ) * share_rows + gathered_row % share_rows
    first_source, second_source, _ = pair_orbitals(source_slot, occ_slots, occ_cap, sym_count)
    source_ok = is_orbital(occupied_count, first_source, occ_cap) & is_orbital(
        occupied_count, second_source, occ_cap
    )
    contract_slot = col_number * tile_width + jnp.arange(tile_width, dtype=jnp.int32)
    first_contract, second_contract, _ = pair_orbitals(
        contract_slot, virt_slots, virt_cap, sym_count
    )
    contract_ok = is_orbital(virtual_count, first_contract, virt_cap) & is_orbital(
        virtual_count, second_contract, virt_cap
    )
    masked = jnp.where(
        source_ok[:, :, None] & contract_ok[:, None, :], gathered, jnp.zeros((), gathered.dtype)
    )
    summed = lax.psum_scatter(
        jnp.einsum("sqd,spd->qsp", masked, integrals, preferred_element_type=jnp.float32),
        "col",
        scatter_dimension=0,
        tiled=True,
    )
    ladder = summed.transpose(1, 0, 2)
    row_base = (2 * col_number + occ_number) * share_rows
    output_slot = row_base + jnp.arange(share_rows, dtype=jnp.int32)
    first_occupied, second_occupied, occupied_mate = pair_orbitals(
        output_slot, occ_slots, occ_cap, sym_count
    )
    col_base = row_number * tile_width
    output_pair = col_base + jnp.arange(tile_width, dtype=jnp.int32)
    first_virtual, second_virtual, virtual_mate = pair_orbitals(
        output_pair, virt_slots, virt_cap, sym_count
    )
    mirrored = jax.vmap(mirror_block)(ladder, occupied_mate - row_base, virtual_mate - col_base)
    symmetrized = ladder + mirrored
    hole_ok = is_orbital(occupied_count, first_occupied, occ_cap) & is_orbital(
        occupied_count, second_occupied, occ_cap
    )
    pair_ok = is_orbital(virtual_count, first_virtual, virt_cap) & is_orbital(
        virtual_count, second_virtual, virt_cap
    )
    pair_energy = table_value(virtual_energy, first_virtual) + table_value(
        virtual_energy, second_virtual
    )
    hole_energy = table_value(occupied_energy, first_occupied) + table_value(
        occupied_energy, second_occupied
    )
    denominator = pair_energy[:, None, :] - hole_energy[:, :, None]
    allowed = hole_ok[:, :, None] & pair_ok[:, None, :]
    return jnp.where(allowed, symmetrized / denominator, jnp.zeros((), jnp.float32))


class Plan:
    def __init__(self, amp_shape, int_shape, rows, virt_slots, occ_slots):
        self.syms, self.share, self.width = amp_shape
        self.pairs = int_shape[1]
        self.rows = rows
        self.virt_slots, self.occ_slots = virt_slots, occ_slots
        self.virt_cap, self.occ_cap = virt_slots // 8, occ_slots // 8
        self.tiles = self.width // LANES
        self.row_tiles = self.share // TILE_ROWS
        self.pay_tiles = self.syms * self.tiles * self.row_tiles
        self.pay_room = self.pay_tiles * TILE_ROWS + self.share
        self.enc_tiles = (self.share // 2 + self.occ_slots // 2) // TILE_ROWS
        self.at_ndt = 2
        self.at_first = self.at_ndt + 2 * self.syms
        self.at_reps = self.at_first + 2 * self.syms * self.tiles
        self.at_self = self.at_reps + self.syms * rows
        self.at_more = self.at_self + self.syms * rows
        self.base_tiles = self.pay_tiles * 43 // 64
        self.enc_shape = (self.enc_tiles * TILE_ROWS, self.pairs + LANES)


def row_counts(plan, tab, sym, share):
    reps = tab[plan.at_reps + sym * plan.rows + share]
    selfs = tab[plan.at_self + sym * plan.rows + share]
    return reps, selfs, padded(2 * reps + selfs)


def band(rel_row):
    return (lax.broadcasted_iota(I32, (2 * LANES, LANES), 0) == rel_row).astype(BF16)


def pack_kernel(plan, tab, amp, dest, rel, pay, acc):
    pay[...] = jnp.zeros_like(pay)
    row = tab[0]
    base = jnp.int32(0)
    for sym in range(plan.syms):
        _, _, nrt = row_counts(plan, tab, sym, row)
        ndt = tab[plan.at_ndt + sym]
        pick = (
            lax.broadcasted_iota(I32, (plan.share, plan.share), 0) == dest[sym : sym + 1, :]
        ).astype(BF16)
        compact = jnp.dot(pick, amp[sym], preferred_element_type=F32).astype(BF16)
        acc[...] = jnp.zeros_like(acc)
        for tile in range(plan.tiles):
            at = sym * plan.tiles + tile
            placed = lax.dot_general(
                compact[:, tile * LANES : (tile + 1) * LANES],
                band(rel[at : at + 1, :]),
                (((1,), (1,)), ((), ())),
                preferred_element_type=F32,
            )
            first = tab[plan.at_first + at]
            acc[first] += placed[:, :LANES]
            acc[first + 1] += placed[:, LANES:]

        def put(tile, _, base=base, nrt=nrt):
            start = pl.multiple_of((base + tile * nrt) * TILE_ROWS, TILE_ROWS)
            pay[pl.ds(start, plan.share), :] = acc[tile].astype(BF16)
            return 0

        lax.fori_loop(0, ndt, put, 0)
        base = base + nrt * ndt


def pack(plan, tab, amp, dest, rel):
    vm = pl.BlockSpec(memory_space=pltpu.VMEM)
    return pl.pallas_call(
        functools.partial(pack_kernel, plan),
        out_shape=jax.ShapeDtypeStruct((plan.pay_room, LANES), BF16),
        in_specs=[pl.BlockSpec(memory_space=pltpu.SMEM), vm, vm, vm],
        out_specs=vm,
        scratch_shapes=[pltpu.VMEM((plan.tiles + 1, plan.share, LANES), F32)],
        compiler_params=pltpu.CompilerParams(vmem_limit_bytes=40 << 20),
        name="pack",
    )(tab, amp, dest, rel)


def share_of(plan, row, kind):
    step, side = kind
    if step == 0:
        return row, row >= 0
    if side == "right":
        return row - step, row >= step
    if side == "left":
        return row + step, row + step < plan.rows
    share = jnp.where(row >= plan.rows // 2, row - step, row + step)
    return share, (share >= 0) & (share < plan.rows)


def lane_mates(plan, rows, sym, fbase, tile):
    flip = sym * plan.virt_cap + fbase + (tile * LANES) // plan.virt_slots
    return lax.broadcasted_iota(I32, (rows, LANES), 1) ^ flip


def lane_take(x, index):
    return jnp.take_along_axis(x, index, axis=1)


def ladder_kernel(plan, kind, count, pay_rows, tab, rel, *refs):
    pays, (rest, ints, sib_ints) = refs[:count], refs[count : count + 3]
    outs, (pay, held, dense, prod, enc, sems, int_sems) = refs[-7 - plan.rows : -7], refs[-7:]
    row, col = tab[0], tab[1]
    sym = lax.rem(col, 2)
    share, active = share_of(plan, row, kind)
    steps = held.shape[1]
    ptile = plan.pairs // steps

    def int_copies(pt):
        return [
            pltpu.make_async_copy(
                ref.at[sym, pl.ds(pt * ptile, ptile)], held.at[part, pt], int_sems.at[part, pt]
            )
            for part, ref in enumerate((ints, sib_ints))
        ]

    def pay_copies(pair):
        return [
            pltpu.make_async_copy(ref, pay.at[part, pl.ds(0, pay_rows)], sems.at[part])
            for part, ref in enumerate(pair)
        ]

    @pl.when(active)
    def _():
        for start in (pay_rows, plan.pay_room - plan.share):
            pay[:, start : start + plan.share, :] = jnp.zeros((2, plan.share, LANES), BF16)
        if count == 2:
            for copy in pay_copies(pays):
                copy.start()
        else:
            upper = row >= plan.rows // 2

            @pl.when(upper)
            def _():
                for copy in pay_copies(pays[:2]):
                    copy.start()

            @pl.when(jnp.logical_not(upper))
            def _():
                for copy in pay_copies(pays[2:]):
                    copy.start()

        for copy in pay_copies(pays[:2]):
            copy.wait()
        for pt in range(steps):
            for copy in int_copies(pt):
                copy.start()

        @pl.when(tab[plan.at_more] > 0)
        def _():
            for part in range(2):
                copy = pltpu.make_async_copy(
                    rest.at[part, share], pay.at[part, pl.ds(pay_rows, rest.shape[2])], sems.at[part]
                )
                copy.start()
                copy.wait()

        reps, selfs, nrt = row_counts(plan, tab, sym, share)
        _, _, nrt0 = row_counts(plan, tab, 0, share)
        rep_room = padded(reps) * TILE_ROWS
        lines = lax.broadcasted_iota(I32, (plan.share, plan.share), 1)
        spread = lines + jnp.where(lines < reps, 0, jnp.where(lines < 2 * reps, 1, 2)) * (
            rep_room - reps
        )
        spread = jnp.where(
            spread == lax.broadcasted_iota(I32, (plan.share, plan.share), 0), 1.0, 0.0
        ).astype(BF16)
        group = 4
        for part in range(2):
            ndt0 = tab[plan.at_ndt + part * plan.syms]
            ndt = tab[plan.at_ndt + part * plan.syms + sym]
            base = jnp.where(sym == 0, 0, nrt0 * ndt0)
            for at_tile in range(0, plan.tiles, group):
                filled = []
                for tile in range(at_tile, at_tile + group):
                    at = (part * plan.syms + sym) * plan.tiles + tile
                    first = tab[plan.at_first + at]
                    pieces = []
                    for step in range(2):
                        use = jnp.maximum(jnp.minimum(first + step, ndt - 1), 0)
                        start = pl.multiple_of((base + use * nrt) * TILE_ROWS, TILE_ROWS)
                        pieces.append(pay[part, pl.ds(start, plan.share), :])
                    filled.append(
                        jnp.dot(
                            jnp.concatenate(pieces, axis=1),
                            band(rel[pl.ds(at, 1), :]),
                            preferred_element_type=F32,
                        ).astype(BF16)
                    )
                dense[part, :, at_tile * LANES : (at_tile + group) * LANES] = jnp.dot(
                    spread, jnp.concatenate(filled, axis=1), preferred_element_type=F32
                ).astype(BF16)

        def multiply(pt, _):
            for copy in int_copies(pt):
                copy.wait()
            prod[:, pl.ds(pl.multiple_of(pt * ptile, ptile), ptile)] = lax.dot_general(
                dense[0], held[0, pt], (((1,), (1,)), ((), ())), preferred_element_type=F32
            ) + lax.dot_general(
                dense[1], held[1, pt], (((1,), (1,)), ((), ())), preferred_element_type=F32
            )
            return 0

        lax.fori_loop(0, steps, multiply, 0)

        fbase = row * (plan.pairs // plan.virt_slots)

        def chunk(k, _):
            to_row = pl.multiple_of(k * TILE_ROWS, TILE_ROWS)
            mate_row = pl.multiple_of(to_row + rep_room, TILE_ROWS)
            own_row = pl.multiple_of(jnp.where(to_row < rep_room, to_row, mate_row), TILE_ROWS)
            sums, top = [], None
            for v in range(plan.pairs // LANES):
                lanes = slice(v * LANES, (v + 1) * LANES)
                mirrored = lane_take(
                    prod[pl.ds(mate_row, TILE_ROWS), lanes],
                    lane_mates(plan, TILE_ROWS, sym, fbase, v),
                )
                both = prod[pl.ds(own_row, TILE_ROWS), lanes] + mirrored
                sums.append(both)
                top = jnp.abs(both) if top is None else jnp.maximum(top, jnp.abs(both))
            peak = jnp.maximum(jnp.max(top, axis=1, keepdims=True), 1e-30)
            power = jnp.floor(jnp.log2(32000.0 / peak))
            scale = jnp.exp2(power)
            for v, both in enumerate(sums):
                enc[pl.ds(to_row, TILE_ROWS), v * LANES : (v + 1) * LANES] = (
                    jnp.round(both * scale).astype(I32).astype(I16)
                )
            enc[pl.ds(to_row, TILE_ROWS), plan.pairs :] = (
                jnp.broadcast_to(power, (TILE_ROWS, LANES)).astype(I32).astype(I16)
            )
            return 0

        lax.fori_loop(0, padded(reps) + padded(selfs), chunk, 0)

        for flip, out in enumerate(outs):

            @pl.when((col ^ share) == flip)
            def _():
                copy = pltpu.make_async_copy(enc, out, sems.at[0])
                copy.start()
                copy.wait()


def ladder_call(plan, kind, tab, rel, pays, rest, integrals, sib_integrals, encs):
    steps = 4
    n = plan.rows
    smem, vmem = (pl.BlockSpec(memory_space=space) for space in (pltpu.SMEM, pltpu.VMEM))
    first_enc = 5 + len(pays)
    return pl.pallas_call(
        functools.partial(ladder_kernel, plan, kind, len(pays), pays[0].shape[0]),
        out_shape=[jax.ShapeDtypeStruct(plan.enc_shape, I16)] * n,
        in_specs=[smem, vmem] + [ANY] * (len(pays) + 3 + len(encs)),
        out_specs=[ANY] * n,
        scratch_shapes=[
            pltpu.VMEM((2, plan.pay_room, LANES), BF16),
            pltpu.VMEM((2, steps, plan.pairs // steps, plan.width), BF16),
            pltpu.VMEM((2, plan.share, plan.width), BF16),
            pltpu.VMEM((plan.share, plan.pairs), F32),
            pltpu.VMEM(plan.enc_shape, I16),
            pltpu.SemaphoreType.DMA((2,)),
            pltpu.SemaphoreType.DMA((2, steps)),
        ],
        input_output_aliases={first_enc + i: i for i in range(len(encs))},
        compiler_params=pltpu.CompilerParams(vmem_limit_bytes=48 << 20),
        cost_estimate=pl.CostEstimate(
            flops=2 * plan.syms * plan.share * plan.width * plan.pairs,
            bytes_accessed=2 * plan.syms * plan.width * plan.pairs,
            transcendentals=0,
        ),
        name="ladder",
    )(tab, rel, *pays, rest, integrals, sib_integrals, *encs)


def finish_kernel(plan, wtile, tab, line, hole, pair, pair_ok, *refs):
    n = plan.rows
    out, held, pick, sems = refs[-4:]
    away_sets = [refs[n * i : n * (i + 1)] for i in range(n - 1)]
    step = pl.program_id(0)
    row, col = tab[0], tab[1]
    core = lax.rem(col, 2)

    def fetch(sources):
        parts = [(core, 0), (1 - core, 0), (core, 1), (1 - core, 1)]
        copies = [
            pltpu.make_async_copy(ref, held.at[sym, side], sems.at[number])
            for number, (ref, (sym, side)) in enumerate(zip(sources, parts))
        ]
        for copy in copies:
            copy.start()
        places = lax.broadcasted_iota(I32, pick.shape[2:], 1)
        for sym in range(plan.syms):
            for half in range(2):
                pick[sym, half] = (places + half * pick.shape[3] == line[sym]).astype(BF16)
        for copy in copies:
            copy.wait()

    which = jnp.maximum(jnp.abs(row - col) - 1, 0)
    for number, sources in enumerate(away_sets):

        @pl.when((step == 0) & (which == number))
        def _(sources=sources):
            fetch(sources)

    fbase = row * (plan.pairs // plan.virt_slots) + step * (wtile // plan.virt_slots)
    for sym in range(plan.syms):
        count = plan.enc_shape[0] if sym == 0 else plan.share // 2
        reps, selfs, _ = row_counts(plan, tab, sym, col)
        live = lax.broadcasted_iota(I32, (count, LANES), 0) < (
            padded(reps) + padded(selfs)
        ) * TILE_ROWS
        scales = [
            jnp.exp2(
                -held[sym, side, pl.ds(0, count), pl.ds(plan.pairs, LANES)].astype(I32).astype(F32)
            )
            for side in range(2)
        ]
        terms = [[], []]
        for v in range(wtile // LANES):
            lanes = pl.ds(pl.multiple_of(step * wtile + v * LANES, LANES), LANES)
            left = jnp.where(
                live,
                held[sym, 0, pl.ds(0, count), lanes].astype(I32).astype(F32) * scales[0]
                + held[sym, 1, pl.ds(0, count), lanes].astype(I32).astype(F32) * scales[1],
                0.0,
            )
            for term in terms:
                term.append(left.astype(BF16))
                left = left - term[-1].astype(F32)
        terms = [jnp.concatenate(term, axis=1) for term in terms]
        halves = []
        for half in range(2):
            total = None
            for term in terms:
                part = jnp.dot(pick[sym, half, :, :count], term, preferred_element_type=F32)
                total = part if total is None else total + part
            halves.append(total)
        for v in range(wtile // LANES):
            lanes = slice(v * LANES, (v + 1) * LANES)
            result = halves[0][:, lanes] + lane_take(
                halves[1][:, lanes], lane_mates(plan, plan.share, sym, fbase, v)
            )
            allowed = (line[sym] >= 0) & (pair_ok[sym, :, lanes] > 0)
            out[sym, :, lanes] = jnp.where(
                allowed, result / (pair[sym, :, lanes] - hole[sym]), 0.0
            )


def finish(plan, tab, line, hole, pair, pair_ok, sources):
    wtile = min(256, plan.pairs)
    whole = lambda shape: pl.BlockSpec(shape, lambda i, tab: (0,) * len(shape))
    tiled = pl.BlockSpec((plan.syms, 1, wtile), lambda i, tab: (0, 0, i))
    grid_spec = pltpu.PrefetchScalarGridSpec(
        num_scalar_prefetch=1,
        grid=(plan.pairs // wtile,),
        in_specs=[whole(line.shape), whole(hole.shape), tiled, tiled] + [ANY] * len(sources),
        out_specs=pl.BlockSpec((plan.syms, plan.share, wtile), lambda i, tab: (0, 0, i)),
        scratch_shapes=[
            pltpu.VMEM((plan.syms, 2) + plan.enc_shape, I16),
            pltpu.VMEM((plan.syms, 2, plan.share, plan.enc_shape[0]), BF16),
            pltpu.SemaphoreType.DMA((4,)),
        ],
    )
    return pl.pallas_call(
        functools.partial(finish_kernel, plan, wtile),
        out_shape=jax.ShapeDtypeStruct((plan.syms, plan.share, plan.pairs), F32),
        grid_spec=grid_spec,
        compiler_params=pltpu.CompilerParams(
            dimension_semantics=("arbitrary",), vmem_limit_bytes=48 << 20
        ),
        name="finish",
    )(tab, line, hole, pair, pair_ok, *sources)


def occupied_share(plan, counts, share_number):
    slot = share_number * plan.share + jnp.arange(plan.share, dtype=I32)
    first, second, mate = pair_orbitals(slot, plan.occ_slots, plan.occ_cap, plan.syms)
    ok = is_orbital(counts, first, plan.occ_cap) & is_orbital(counts, second, plan.occ_cap)
    lead = jnp.minimum(slot[None, :], mate)
    is_rep = ok & (first < second)
    is_self = ok & (first == second)
    before = slot[None, None, :] < lead[:, :, None]
    rank = jnp.sum((is_rep[:, None, :] & before).astype(I32), axis=-1)
    self_rank = jnp.sum((is_self[:, None, :] & before).astype(I32), axis=-1)
    return first, second, ok, is_rep, is_self, rank, self_rank


def padded(count):
    return (count + TILE_ROWS - 1) // TILE_ROWS


def line_tables(plan, virtual_energy, occupied_energy, virtual_count, occupied_count):
    row = lax.axis_index("row")
    col = lax.axis_index("col")
    occ = lax.axis_index("occ")
    syms = plan.syms
    slots = jnp.arange(2 * plan.rows * plan.share, dtype=I32)
    first, second, _ = pair_orbitals(slots, plan.occ_slots, plan.occ_cap, syms)
    ok = is_orbital(occupied_count, first, plan.occ_cap) & is_orbital(
        occupied_count, second, plan.occ_cap
    )
    grouped = lambda x: jnp.sum(x.astype(I32).reshape(syms, plan.rows, 2, plan.share), axis=-1)
    reps_all = grouped(ok & (first < second))
    selfs_all = grouped(ok & (first == second))
    reps = jnp.where(occ == 0, reps_all[:, :, 0], reps_all[:, :, 1])
    selfs = jnp.where(occ == 0, selfs_all[:, :, 0], selfs_all[:, :, 1])
    blocks = plan.rows
    slots = jnp.arange(blocks * plan.width, dtype=I32)
    first, second, _ = pair_orbitals(slots, plan.virt_slots, plan.virt_cap, syms)
    ok = is_orbital(virtual_count, first, plan.virt_cap) & is_orbital(
        virtual_count, second, plan.virt_cap
    )
    per_block = jnp.sum(ok.astype(I32).reshape(syms, blocks, plan.width), axis=-1)
    ndt_all = (per_block + LANES - 1) // LANES
    tiles_needed = jnp.max(
        jnp.sum(padded(2 * reps_all + selfs_all)[:, :, :, None] * ndt_all[:, None, None, :], axis=0)
    )
    more = (tiles_needed > plan.base_tiles).astype(I32)
    slot = (col ^ jnp.arange(2, dtype=I32))[:, None] * plan.width + jnp.arange(
        plan.width, dtype=I32
    )
    first, second, _ = pair_orbitals(slot.reshape(-1), plan.virt_slots, plan.virt_cap, syms)
    ok = is_orbital(virtual_count, first, plan.virt_cap) & is_orbital(
        virtual_count, second, plan.virt_cap
    )
    ok = jnp.swapaxes(ok.reshape(syms, 2, plan.tiles, LANES), 0, 1)
    per_tile = jnp.sum(ok.astype(I32), axis=-1)
    tile_ids = jnp.arange(plan.tiles, dtype=I32)
    starts = jnp.sum(
        jnp.where(tile_ids[None, :] < tile_ids[:, None], per_tile[:, :, None, :], 0), axis=-1
    )
    lane_ids = jnp.arange(LANES, dtype=I32)
    within = jnp.sum(
        (ok[..., None, :] & (lane_ids[None, :] < lane_ids[:, None])).astype(I32), axis=-1
    )
    firsts = starts // LANES
    rel = jnp.where(ok, within + (starts % LANES)[..., None], -1)
    ndt = (jnp.sum(per_tile, axis=-1) + LANES - 1) // LANES
    tab = jnp.concatenate(
        [
            jnp.stack([row, col]).astype(I32),
            ndt.reshape(-1),
            firsts.reshape(-1),
            reps.reshape(-1),
            selfs.reshape(-1),
            more[None],
        ]
    )
    _, _, ok, is_rep, is_self, rank, self_rank = occupied_share(
        plan, occupied_count, 2 * row + occ
    )
    n_rep = jnp.sum(is_rep.astype(I32), axis=-1, keepdims=True)
    dest = jnp.where(is_self, 2 * n_rep + self_rank, jnp.where(is_rep, rank, n_rep + rank))
    dest = jnp.where(ok, dest, -1)
    first, second, ok, is_rep, is_self, rank, self_rank = occupied_share(
        plan, occupied_count, 2 * col + occ
    )
    n_rep = jnp.sum(is_rep.astype(I32), axis=-1, keepdims=True)
    count = plan.enc_tiles * TILE_ROWS
    rep_room = padded(n_rep) * TILE_ROWS
    line = jnp.where(is_self, rep_room + self_rank, jnp.where(is_rep, rank, count + rank))
    line = jnp.where(ok, line, -1)
    hole = table_value(occupied_energy, first) + table_value(occupied_energy, second)
    slot = row * plan.pairs + jnp.arange(plan.pairs, dtype=I32)
    first, second, _ = pair_orbitals(slot, plan.virt_slots, plan.virt_cap, syms)
    pair_ok = is_orbital(virtual_count, first, plan.virt_cap) & is_orbital(
        virtual_count, second, plan.virt_cap
    )
    pair = table_value(virtual_energy, first) + table_value(virtual_energy, second)
    return (
        more,
        tab,
        dest,
        rel.reshape(2 * syms * plan.tiles, LANES),
        line[:, :, None],
        hole[:, :, None],
        pair[:, None, :],
        pair_ok.astype(I32)[:, None, :],
    )


def to_roots(plan, encs, distances):
    received = [encs[0]]
    for flip in range(1, plan.rows):
        pairs = [
            (row * plan.rows + (root ^ flip), row * plan.rows + root)
            for row in range(plan.rows)
            for root in range(plan.rows)
            if abs(row - root) in distances
        ]
        received.append(lax.ppermute(encs[flip], ("row", "col"), pairs))
    return received


def on_device_line(
    rows, amplitudes, integrals, virtual_energy, occupied_energy, virtual_count, occupied_count
):
    n = rows
    plan = Plan(
        amplitudes.shape, integrals.shape, rows, virtual_energy.shape[0], occupied_energy.shape[0]
    )
    swap = [(i, i ^ 1) for i in range(n)]
    sibling = lambda x: lax.ppermute(x, "col", swap)
    sib_integrals = sibling(integrals)
    more, tab, dest, rel, line, hole, pair, pair_ok = line_tables(
        plan, virtual_energy, occupied_energy, virtual_count, occupied_count
    )
    packed = pack(plan, tab, amplitudes, dest, rel)
    base_rows = plan.base_tiles * TILE_ROWS
    all_rows = plan.pay_tiles * TILE_ROWS
    pay = packed[:base_rows]

    def send_rest(packed):
        gathered = lax.all_gather(packed[base_rows:all_rows], "row")
        return jnp.stack([gathered, sibling(gathered)])

    def no_rest(packed):
        return jnp.zeros((2, n, all_rows - base_rows, LANES), BF16)

    rest = lax.cond(more > 0, send_rest, no_rest, packed)
    row = lax.axis_index("row")

    def work(kind, pays, encs):
        both = [x for pay in pays for x in (pay, sibling(pay))]
        return ladder_call(plan, kind, tab, rel, both, rest, integrals, sib_integrals, encs)

    right = lax.ppermute(pay, "row", [(i, i + 1) for i in range(n - 1)])
    left = lax.ppermute(pay, "row", [(i + 1, i) for i in range(n - 1)])
    encs = work((0, ""), [pay], [])
    sources = []
    for step in range(2, n):
        right, left, encs = lax.optimization_barrier((right, left, encs))
        if step < n - 1:
            ahead = (
                lax.ppermute(right, "row", [(i, i + 1) for i in range(step - 1, n - 1)]),
                lax.ppermute(left, "row", [(i + 1, i) for i in range(0, n - step)]),
            )
        else:
            last = jnp.where(row >= n // 2, right, left)
            last = lax.ppermute(last, "row", [(n - 2, n - 1), (1, 0)])
        if step == 2:
            encs = work((1, "right"), [right], encs)
            encs = work((1, "left"), [left], encs)
        else:
            sources += to_roots(plan, encs, (0, 1) if step == 3 else (step - 2,))
            encs = work((step - 1, ""), [right, left], [])
        if step < n - 1:
            right, left = ahead
    sources += to_roots(plan, encs, (n - 2,))
    last, sources = lax.optimization_barrier((last, sources))
    sources += to_roots(plan, work((n - 1, ""), [last], []), (n - 1,))
    return finish(plan, tab, line, hole, pair, pair_ok, sources)


def solution(mesh):
    rows, cols = mesh.shape["row"], mesh.shape["col"]
    placed = (P(None, ("row", "occ"), "col"), P(None, "row", "col"), P(), P(), P(), P())
    on_device = on_device_general
    if rows == 4 and cols == 4:
        on_device = functools.partial(on_device_line, rows)
    return jax.shard_map(
        on_device,
        mesh=mesh,
        in_specs=placed,
        out_specs=P(None, ("col", "occ"), "row"),
        check_vma=False,
    )
```

```python
import functools
import jax
import jax.numpy as jnp
from jax import lax
from jax.experimental import pallas as pl
from jax.experimental.pallas import tpu as pltpu
from jax.sharding import PartitionSpec as P

F32, BF16, I32, I16 = jnp.float32, jnp.bfloat16, jnp.int32, jnp.int16
LANES = 128
TILE_ROWS = 16
ANY = pl.BlockSpec(memory_space=pl.ANY)


def table_value(values_table, positions):
    places = jnp.arange(values_table.shape[0], dtype=jnp.int32)
    matches = positions[..., None] == places
    return jnp.sum(jnp.where(matches, values_table, jnp.zeros((), values_table.dtype)), axis=-1)


def is_orbital(counts, orbital, capacity):
    return orbital % capacity < table_value(counts, orbital // capacity)


def pair_orbitals(slot, group_width, capacity, sym_count):
    symmetry = jnp.arange(sym_count, dtype=jnp.int32)[:, None]
    offset = slot // group_width
    first_orb = jnp.broadcast_to(slot % group_width, (sym_count, slot.shape[0]))
    second_orb = jnp.bitwise_xor(first_orb, symmetry * capacity + offset[None, :])
    mate = offset[None, :] * group_width + second_orb
    return (first_orb, second_orb, mate)


def mirror_block(block, row_index, col_index):
    return jnp.take(jnp.take(block, row_index, axis=0), col_index, axis=1)


def on_device_general(
    amplitudes, integrals, virtual_energy, occupied_energy, virtual_count, occupied_count
):
    row_number = lax.axis_index("row")
    col_number = lax.axis_index("col")
    occ_number = lax.axis_index("occ")
    sym_count = amplitudes.shape[0]
    share_rows = amplitudes.shape[1]
    tile_width = amplitudes.shape[2]
    virt_slots = virtual_energy.shape[0]
    occ_slots = occupied_energy.shape[0]
    virt_cap = virt_slots // 8
    occ_cap = occ_slots // 8
    gathered = lax.all_gather(amplitudes, "row", axis=1, tiled=True)
    gathered_row = jnp.arange(gathered.shape[1], dtype=jnp.int32)
    source_slot = (
        2 * (gathered_row // share_rows) + occ_number
    ) * share_rows + gathered_row % share_rows
    first_source, second_source, _ = pair_orbitals(source_slot, occ_slots, occ_cap, sym_count)
    source_ok = is_orbital(occupied_count, first_source, occ_cap) & is_orbital(
        occupied_count, second_source, occ_cap
    )
    contract_slot = col_number * tile_width + jnp.arange(tile_width, dtype=jnp.int32)
    first_contract, second_contract, _ = pair_orbitals(
        contract_slot, virt_slots, virt_cap, sym_count
    )
    contract_ok = is_orbital(virtual_count, first_contract, virt_cap) & is_orbital(
        virtual_count, second_contract, virt_cap
    )
    masked = jnp.where(
        source_ok[:, :, None] & contract_ok[:, None, :], gathered, jnp.zeros((), gathered.dtype)
    )
    summed = lax.psum_scatter(
        jnp.einsum("sqd,spd->qsp", masked, integrals, preferred_element_type=jnp.float32),
        "col",
        scatter_dimension=0,
        tiled=True,
    )
    ladder = summed.transpose(1, 0, 2)
    row_base = (2 * col_number + occ_number) * share_rows
    output_slot = row_base + jnp.arange(share_rows, dtype=jnp.int32)
    first_occupied, second_occupied, occupied_mate = pair_orbitals(
        output_slot, occ_slots, occ_cap, sym_count
    )
    col_base = row_number * tile_width
    output_pair = col_base + jnp.arange(tile_width, dtype=jnp.int32)
    first_virtual, second_virtual, virtual_mate = pair_orbitals(
        output_pair, virt_slots, virt_cap, sym_count
    )
    mirrored = jax.vmap(mirror_block)(ladder, occupied_mate - row_base, virtual_mate - col_base)
    symmetrized = ladder + mirrored
    hole_ok = is_orbital(occupied_count, first_occupied, occ_cap) & is_orbital(
        occupied_count, second_occupied, occ_cap
    )
    pair_ok = is_orbital(virtual_count, first_virtual, virt_cap) & is_orbital(
        virtual_count, second_virtual, virt_cap
    )
    pair_energy = table_value(virtual_energy, first_virtual) + table_value(
        virtual_energy, second_virtual
    )
    hole_energy = table_value(occupied_energy, first_occupied) + table_value(
        occupied_energy, second_occupied
    )
    denominator = pair_energy[:, None, :] - hole_energy[:, :, None]
    allowed = hole_ok[:, :, None] & pair_ok[:, None, :]
    return jnp.where(allowed, symmetrized / denominator, jnp.zeros((), jnp.float32))


class Plan:
    def __init__(self, amp_shape, int_shape, rows, virt_slots, occ_slots):
        self.syms, self.share, self.width = amp_shape
        self.pairs = int_shape[1]
        self.rows = rows
        self.virt_slots, self.occ_slots = virt_slots, occ_slots
        self.virt_cap, self.occ_cap = virt_slots // 8, occ_slots // 8
        self.tiles = self.width // LANES
        self.row_tiles = self.share // TILE_ROWS
        self.pay_tiles = self.syms * self.tiles * self.row_tiles
        self.pay_room = self.pay_tiles * TILE_ROWS + self.share
        self.enc_tiles = (self.share // 2 + self.occ_slots // 2) // TILE_ROWS
        self.at_ndt = 2
        self.at_first = self.at_ndt + 2 * self.syms
        self.at_reps = self.at_first + 2 * self.syms * self.tiles
        self.at_self = self.at_reps + self.syms * rows
        self.at_more = self.at_self + self.syms * rows
        self.base_tiles = self.pay_tiles * 43 // 64
        enc_rows = self.enc_tiles * TILE_ROWS
        self.enc_shapes = [(enc_rows, self.pairs + LANES)] * rows
        self.far_shapes = self.enc_shapes[:-1] + [(self.share // 2, self.pairs + LANES)]


def row_counts(plan, tab, sym, share):
    reps = tab[plan.at_reps + sym * plan.rows + share]
    selfs = tab[plan.at_self + sym * plan.rows + share]
    return reps, selfs, padded(2 * reps + selfs)


def band(rel_row):
    return (lax.broadcasted_iota(I32, (2 * LANES, LANES), 0) == rel_row).astype(BF16)


def pack_kernel(plan, tab, amp, dest, rel, pay, acc):
    pay[...] = jnp.zeros_like(pay)
    base = jnp.int32(0)
    for sym in range(plan.syms):
        ndt, nrt = tab[sym], tab[plan.syms + sym]
        pick = (
            lax.broadcasted_iota(I32, (plan.share, plan.share), 0) == dest[sym : sym + 1, :]
        ).astype(BF16)
        compact = jnp.dot(pick, amp[sym], preferred_element_type=F32).astype(BF16)
        acc[...] = jnp.zeros_like(acc)
        for tile in range(plan.tiles):
            at = sym * plan.tiles + tile
            placed = lax.dot_general(
                compact[:, tile * LANES : (tile + 1) * LANES],
                band(rel[at : at + 1, :]),
                (((1,), (1,)), ((), ())),
                preferred_element_type=F32,
            )
            first = tab[2 * plan.syms + at]
            acc[first] += placed[:, :LANES]
            acc[first + 1] += placed[:, LANES:]

        def put(tile, _, base=base, nrt=nrt):
            start = pl.multiple_of((base + tile * nrt) * TILE_ROWS, TILE_ROWS)
            pay[pl.ds(start, plan.share), :] = acc[tile].astype(BF16)
            return 0

        lax.fori_loop(0, ndt, put, 0)
        base = base + nrt * ndt


def pack(plan, tab, amp, dest, rel):
    vm = pl.BlockSpec(memory_space=pltpu.VMEM)
    return pl.pallas_call(
        functools.partial(pack_kernel, plan),
        out_shape=jax.ShapeDtypeStruct((plan.pay_room, LANES), BF16),
        in_specs=[pl.BlockSpec(memory_space=pltpu.SMEM), vm, vm, vm],
        out_specs=vm,
        scratch_shapes=[pltpu.VMEM((plan.tiles + 1, plan.share, LANES), F32)],
        compiler_params=pltpu.CompilerParams(vmem_limit_bytes=40 << 20),
        name="pack",
    )(tab, amp, dest, rel)


def share_of(plan, row, kind):
    step, side = kind
    if step == 0:
        return row, row >= 0
    if side == "right":
        return row - step, row >= step
    if side == "left":
        return row + step, row + step < plan.rows
    share = jnp.where(row >= plan.rows // 2, row - step, row + step)
    return share, (share >= 0) & (share < plan.rows)


def lane_mates(plan, rows, sym, fbase, tile):
    flip = sym * plan.virt_cap + fbase + (tile * LANES) // plan.virt_slots
    return lax.broadcasted_iota(I32, (rows, LANES), 1) ^ flip


def lane_take(x, index):
    return jnp.take_along_axis(x, index, axis=1)


def ladder_kernel(plan, kind, count, pay_rows, tab, rel, *refs):
    pays, (rest, ints, sib_ints) = refs[:count], refs[count : count + 3]
    outs, (pay, held, dense, prod, enc, sems, int_sems) = refs[-7 - plan.rows : -7], refs[-7:]
    row, col = tab[0], tab[1]
    sym = lax.rem(col, 2)
    share, active = share_of(plan, row, kind)
    steps = held.shape[1]
    ptile = plan.pairs // steps

    def int_copies(pt):
        return [
            pltpu.make_async_copy(
                ref.at[sym, pl.ds(pt * ptile, ptile)], held.at[part, pt], int_sems.at[part, pt]
            )
            for part, ref in enumerate((ints, sib_ints))
        ]

    def pay_copies(pair):
        return [
            pltpu.make_async_copy(ref, pay.at[part, pl.ds(0, pay_rows)], sems.at[part])
            for part, ref in enumerate(pair)
        ]

    @pl.when(active)
    def _():
        for start in (pay_rows, plan.pay_room - plan.share):
            pay[:, start : start + plan.share, :] = jnp.zeros((2, plan.share, LANES), BF16)
        if count == 2:
            for copy in pay_copies(pays):
                copy.start()
        else:
            upper = row >= plan.rows // 2

            @pl.when(upper)
            def _():
                for copy in pay_copies(pays[:2]):
                    copy.start()

            @pl.when(jnp.logical_not(upper))
            def _():
                for copy in pay_copies(pays[2:]):
                    copy.start()

        for copy in pay_copies(pays[:2]):
            copy.wait()
        for pt in range(steps):
            for copy in int_copies(pt):
                copy.start()

        @pl.when(tab[plan.at_more] > 0)
        def _():
            for part in range(2):
                copy = pltpu.make_async_copy(
                    rest.at[part, share], pay.at[part, pl.ds(pay_rows, rest.shape[2])], sems.at[part]
                )
                copy.start()
                copy.wait()

        reps, selfs, nrt = row_counts(plan, tab, sym, share)
        _, _, nrt0 = row_counts(plan, tab, 0, share)
        rep_room = padded(reps) * TILE_ROWS
        lines = lax.broadcasted_iota(I32, (plan.share, plan.share), 1)
        spread = lines + jnp.where(lines < reps, 0, jnp.where(lines < 2 * reps, 1, 2)) * (
            rep_room - reps
        )
        spread = jnp.where(
            spread == lax.broadcasted_iota(I32, (plan.share, plan.share), 0), 1.0, 0.0
        ).astype(BF16)
        group = 4
        for part in range(2):
            ndt0 = tab[plan.at_ndt + part * plan.syms]
            ndt = tab[plan.at_ndt + part * plan.syms + sym]
            base = jnp.where(sym == 0, 0, nrt0 * ndt0)
            for at_tile in range(0, plan.tiles, group):
                filled = []
                for tile in range(at_tile, at_tile + group):
                    at = (part * plan.syms + sym) * plan.tiles + tile
                    first = tab[plan.at_first + at]
                    pieces = []
                    for step in range(2):
                        use = jnp.maximum(jnp.minimum(first + step, ndt - 1), 0)
                        start = pl.multiple_of((base + use * nrt) * TILE_ROWS, TILE_ROWS)
                        pieces.append(pay[part, pl.ds(start, plan.share), :])
                    filled.append(
                        jnp.dot(
                            jnp.concatenate(pieces, axis=1),
                            band(rel[pl.ds(at, 1), :]),
                            preferred_element_type=F32,
                        ).astype(BF16)
                    )
                dense[part, :, at_tile * LANES : (at_tile + group) * LANES] = jnp.dot(
                    spread, jnp.concatenate(filled, axis=1), preferred_element_type=F32
                ).astype(BF16)

        def multiply(pt, _):
            for copy in int_copies(pt):
                copy.wait()
            prod[:, pl.ds(pl.multiple_of(pt * ptile, ptile), ptile)] = lax.dot_general(
                dense[0], held[0, pt], (((1,), (1,)), ((), ())), preferred_element_type=F32
            ) + lax.dot_general(
                dense[1], held[1, pt], (((1,), (1,)), ((), ())), preferred_element_type=F32
            )
            return 0

        lax.fori_loop(0, steps, multiply, 0)

        fbase = row * (plan.pairs // plan.virt_slots)

        def chunk(k, _):
            to_row = pl.multiple_of(k * TILE_ROWS, TILE_ROWS)
            mate_row = pl.multiple_of(to_row + rep_room, TILE_ROWS)
            own_row = pl.multiple_of(jnp.where(to_row < rep_room, to_row, mate_row), TILE_ROWS)
            sums, top = [], None
            for v in range(plan.pairs // LANES):
                lanes = slice(v * LANES, (v + 1) * LANES)
                mirrored = lane_take(
                    prod[pl.ds(mate_row, TILE_ROWS), lanes],
                    lane_mates(plan, TILE_ROWS, sym, fbase, v),
                )
                both = prod[pl.ds(own_row, TILE_ROWS), lanes] + mirrored
                sums.append(both)
                top = jnp.abs(both) if top is None else jnp.maximum(top, jnp.abs(both))
            peak = jnp.maximum(jnp.max(top, axis=1, keepdims=True), 1e-30)
            power = jnp.floor(jnp.log2(32000.0 / peak))
            scale = jnp.exp2(power)
            for v, both in enumerate(sums):
                enc[pl.ds(to_row, TILE_ROWS), v * LANES : (v + 1) * LANES] = (
                    jnp.round(both * scale).astype(I32).astype(I16)
                )
            enc[pl.ds(to_row, TILE_ROWS), plan.pairs :] = (
                jnp.broadcast_to(power, (TILE_ROWS, LANES)).astype(I32).astype(I16)
            )
            return 0

        lax.fori_loop(0, padded(reps) + padded(selfs), chunk, 0)

        flip = col ^ share
        slot = flip if kind[0] < 2 else jnp.where(flip < 2, flip, 2 + sym)
        for number, out in enumerate(outs):

            @pl.when(slot == number)
            def _(out=out):
                copy = pltpu.make_async_copy(enc.at[pl.ds(0, out.shape[0])], out, sems.at[0])
                copy.start()
                copy.wait()


def ladder_call(plan, kind, tab, rel, pays, rest, integrals, sib_integrals, encs):
    steps = 4
    n = plan.rows
    smem, vmem = (pl.BlockSpec(memory_space=space) for space in (pltpu.SMEM, pltpu.VMEM))
    first_enc = 5 + len(pays)
    return pl.pallas_call(
        functools.partial(ladder_kernel, plan, kind, len(pays), pays[0].shape[0]),
        out_shape=[
            jax.ShapeDtypeStruct(shape, I16)
            for shape in (plan.enc_shapes if kind[0] < 2 else plan.far_shapes)
        ],
        in_specs=[smem, vmem] + [ANY] * (len(pays) + 3 + len(encs)),
        out_specs=[ANY] * n,
        scratch_shapes=[
            pltpu.VMEM((2, plan.pay_room, LANES), BF16),
            pltpu.VMEM((2, steps, plan.pairs // steps, plan.width), BF16),
            pltpu.VMEM((2, plan.share, plan.width), BF16),
            pltpu.VMEM((plan.share, plan.pairs), F32),
            pltpu.VMEM(plan.enc_shapes[0], I16),
            pltpu.SemaphoreType.DMA((2,)),
            pltpu.SemaphoreType.DMA((2, steps)),
        ],
        input_output_aliases={first_enc + i: i for i in range(len(encs))},
        compiler_params=pltpu.CompilerParams(vmem_limit_bytes=34 << 20),
        cost_estimate=pl.CostEstimate(
            flops=2 * plan.syms * plan.share * plan.width * plan.pairs,
            bytes_accessed=2 * plan.syms * plan.width * plan.pairs,
            transcendentals=0,
        ),
        name="ladder",
    )(tab, rel, *pays, rest, integrals, sib_integrals, *encs)


def finish_kernel(plan, numbers, wtile, tab, line, hole, pair, pair_ok, *refs):
    n = plan.rows
    out, held, pick, whole, sems, out_sems = refs[-6:]
    row, col = tab[0], tab[1]
    core = lax.rem(col, 2)
    which = jnp.maximum(jnp.abs(row - col) - 1, 0)
    steps = plan.pairs // wtile

    def fetch(sources, by_sym):
        parts = [(core, 0), (1 - core, 0)] + ([(0, 1), (1, 1)] if by_sym else [(core, 1), (1 - core, 1)])
        copies = [
            pltpu.make_async_copy(
                ref, held.at[sym, side, pl.ds(0, ref.shape[0])], sems.at[number]
            )
            for number, (ref, (sym, side)) in enumerate(zip(sources, parts))
        ]
        for copy in copies:
            copy.start()
        places = lax.broadcasted_iota(I32, pick.shape[2:], 1)
        for sym in range(plan.syms):
            for half in range(2):
                pick[sym, half] = (places + half * pick.shape[3] == line[sym, :, 0:1]).astype(BF16)
        for copy in copies:
            copy.wait()

    for place, number in enumerate(numbers):

        @pl.when(which == number)
        def _(sources=refs[n * place : n * (place + 1)], by_sym=number > 0):
            fetch(sources, by_sym)

    def put(step):
        lanes = pl.ds(pl.multiple_of(step * wtile, wtile), wtile)
        return pltpu.make_async_copy(whole.at[:, :, lanes], out.at[:, :, lanes], out_sems.at[step])

    def tile(step, _):
        fbase = row * (plan.pairs // plan.virt_slots) + step * (wtile // plan.virt_slots)
        for sym in range(plan.syms):
            count = plan.enc_shapes[0][0] if sym == 0 else plan.share // 2
            reps, selfs, _ = row_counts(plan, tab, sym, col)
            live = lax.broadcasted_iota(I32, (count, LANES), 0) < (
                padded(reps) + padded(selfs)
            ) * TILE_ROWS
            scales = [
                jnp.exp2(
                    -held[sym, side, pl.ds(0, count), pl.ds(plan.pairs, LANES)]
                    .astype(I32)
                    .astype(F32)
                )
                for side in range(2)
            ]
            spans = [
                pl.ds(pl.multiple_of(step * wtile + v * LANES, LANES), LANES)
                for v in range(wtile // LANES)
            ]
            terms = [[], []]
            for lanes in spans:
                left = jnp.where(
                    live,
                    held[sym, 0, pl.ds(0, count), lanes].astype(I32).astype(F32) * scales[0]
                    + held[sym, 1, pl.ds(0, count), lanes].astype(I32).astype(F32) * scales[1],
                    0.0,
                )
                for term in terms:
                    term.append(left.astype(BF16))
                    left = left - term[-1].astype(F32)
            terms = [jnp.concatenate(term, axis=1) for term in terms]
            halves = []
            for half in range(2):
                total = None
                for term in terms:
                    part = jnp.dot(pick[sym, half, :, :count], term, preferred_element_type=F32)
                    total = part if total is None else total + part
                halves.append(total)
            for v, lanes in enumerate(spans):
                cut = slice(v * LANES, (v + 1) * LANES)
                result = halves[0][:, cut] + lane_take(
                    halves[1][:, cut], lane_mates(plan, plan.share, sym, fbase, v)
                )
                allowed = (line[sym] >= 0) & (pair_ok[sym, :, lanes] > 0)
                whole[sym, :, lanes] = jnp.where(
                    allowed, result / (pair[sym, :, lanes] - hole[sym]), 0.0
                )
        put(step).start()
        return 0

    def drain(step, _):
        put(step).wait()
        return 0

    @pl.when((which >= numbers[0]) & (which <= numbers[-1]))
    def _():
        lax.fori_loop(0, steps, tile, 0)
        lax.fori_loop(0, steps, drain, 0)


def finish(plan, numbers, tab, line, hole, pair, pair_ok, sources, before):
    wtile = min(256, plan.pairs)
    smem, vmem = (pl.BlockSpec(memory_space=space) for space in (pltpu.SMEM, pltpu.VMEM))
    out = jax.ShapeDtypeStruct((plan.syms, plan.share, plan.pairs), F32)
    return pl.pallas_call(
        functools.partial(finish_kernel, plan, numbers, wtile),
        out_shape=out,
        in_specs=[smem] + [vmem] * 4 + [ANY] * (len(sources) + len(before)),
        out_specs=ANY,
        scratch_shapes=[
            pltpu.VMEM((plan.syms, 2) + plan.enc_shapes[0], I16),
            pltpu.VMEM((plan.syms, 2, plan.share, plan.enc_shapes[0][0]), BF16),
            pltpu.VMEM(out.shape, F32),
            pltpu.SemaphoreType.DMA((4,)),
            pltpu.SemaphoreType.DMA((plan.pairs // wtile,)),
        ],
        input_output_aliases={5 + len(sources): 0} if before else {},
        compiler_params=pltpu.CompilerParams(vmem_limit_bytes=30 << 20),
        name="finish",
    )(tab, line, hole, pair, pair_ok, *sources, *before)


def occupied_share(plan, counts, share_number):
    slot = share_number * plan.share + jnp.arange(plan.share, dtype=I32)
    first, second, mate = pair_orbitals(slot, plan.occ_slots, plan.occ_cap, plan.syms)
    ok = is_orbital(counts, first, plan.occ_cap) & is_orbital(counts, second, plan.occ_cap)
    lead = jnp.minimum(slot[None, :], mate)
    is_rep = ok & (first < second)
    is_self = ok & (first == second)
    before = slot[None, None, :] < lead[:, :, None]
    rank = jnp.sum((is_rep[:, None, :] & before).astype(I32), axis=-1)
    self_rank = jnp.sum((is_self[:, None, :] & before).astype(I32), axis=-1)
    return first, second, ok, is_rep, is_self, rank, self_rank


def padded(count):
    return (count + TILE_ROWS - 1) // TILE_ROWS


def line_tables(plan, virtual_energy, occupied_energy, virtual_count, occupied_count):
    row = lax.axis_index("row")
    col = lax.axis_index("col")
    occ = lax.axis_index("occ")
    syms = plan.syms
    slots = jnp.arange(2 * plan.rows * plan.share, dtype=I32)
    first, second, _ = pair_orbitals(slots, plan.occ_slots, plan.occ_cap, syms)
    ok = is_orbital(occupied_count, first, plan.occ_cap) & is_orbital(
        occupied_count, second, plan.occ_cap
    )
    grouped = lambda x: jnp.sum(x.astype(I32).reshape(syms, plan.rows, 2, plan.share), axis=-1)
    reps_all = grouped(ok & (first < second))
    selfs_all = grouped(ok & (first == second))
    reps = jnp.where(occ == 0, reps_all[:, :, 0], reps_all[:, :, 1])
    selfs = jnp.where(occ == 0, selfs_all[:, :, 0], selfs_all[:, :, 1])
    blocks = plan.rows
    slots = jnp.arange(blocks * plan.width, dtype=I32)
    first, second, _ = pair_orbitals(slots, plan.virt_slots, plan.virt_cap, syms)
    ok = is_orbital(virtual_count, first, plan.virt_cap) & is_orbital(
        virtual_count, second, plan.virt_cap
    )
    per_block = jnp.sum(ok.astype(I32).reshape(syms, blocks, plan.width), axis=-1)
    ndt_all = (per_block + LANES - 1) // LANES
    tiles_needed = jnp.max(
        jnp.sum(padded(2 * reps_all + selfs_all)[:, :, :, None] * ndt_all[:, None, None, :], axis=0)
    )
    more = (tiles_needed > plan.base_tiles).astype(I32)
    slot = (col ^ jnp.arange(2, dtype=I32))[:, None] * plan.width + jnp.arange(
        plan.width, dtype=I32
    )
    first, second, _ = pair_orbitals(slot.reshape(-1), plan.virt_slots, plan.virt_cap, syms)
    ok = is_orbital(virtual_count, first, plan.virt_cap) & is_orbital(
        virtual_count, second, plan.virt_cap
    )
    ok = jnp.swapaxes(ok.reshape(syms, 2, plan.tiles, LANES), 0, 1)
    per_tile = jnp.sum(ok.astype(I32), axis=-1)
    tile_ids = jnp.arange(plan.tiles, dtype=I32)
    starts = jnp.sum(
        jnp.where(tile_ids[None, :] < tile_ids[:, None], per_tile[:, :, None, :], 0), axis=-1
    )
    lane_ids = jnp.arange(LANES, dtype=I32)
    within = jnp.sum(
        (ok[..., None, :] & (lane_ids[None, :] < lane_ids[:, None])).astype(I32), axis=-1
    )
    firsts = starts // LANES
    rel = jnp.where(ok, within + (starts % LANES)[..., None], -1)
    ndt = (jnp.sum(per_tile, axis=-1) + LANES - 1) // LANES
    tab = jnp.concatenate(
        [
            jnp.stack([row, col]).astype(I32),
            ndt.reshape(-1),
            firsts.reshape(-1),
            reps.reshape(-1),
            selfs.reshape(-1),
            more[None],
        ]
    )
    _, _, ok, is_rep, is_self, rank, self_rank = occupied_share(
        plan, occupied_count, 2 * row + occ
    )
    n_rep = jnp.sum(is_rep.astype(I32), axis=-1, keepdims=True)
    dest = jnp.where(is_self, 2 * n_rep + self_rank, jnp.where(is_rep, rank, n_rep + rank))
    dest = jnp.where(ok, dest, -1)
    n_valid = jnp.sum(ok.astype(I32), axis=-1)
    pack_tab = jnp.concatenate([ndt[0], padded(n_valid), firsts[0].reshape(-1)])
    first, second, ok, is_rep, is_self, rank, self_rank = occupied_share(
        plan, occupied_count, 2 * col + occ
    )
    n_rep = jnp.sum(is_rep.astype(I32), axis=-1, keepdims=True)
    count = plan.enc_tiles * TILE_ROWS
    rep_room = padded(n_rep) * TILE_ROWS
    line = jnp.where(is_self, rep_room + self_rank, jnp.where(is_rep, rank, count + rank))
    line = jnp.where(ok, line, -1)
    hole = table_value(occupied_energy, first) + table_value(occupied_energy, second)
    slot = row * plan.pairs + jnp.arange(plan.pairs, dtype=I32)
    first, second, _ = pair_orbitals(slot, plan.virt_slots, plan.virt_cap, syms)
    pair_ok = is_orbital(virtual_count, first, plan.virt_cap) & is_orbital(
        virtual_count, second, plan.virt_cap
    )
    pair = table_value(virtual_energy, first) + table_value(virtual_energy, second)
    return (
        more,
        tab,
        pack_tab,
        dest,
        rel.reshape(2 * syms * plan.tiles, LANES),
        jnp.broadcast_to(line[:, :, None], line.shape + (LANES,)),
        jnp.broadcast_to(hole[:, :, None], hole.shape + (LANES,)),
        pair[:, None, :],
        pair_ok.astype(I32)[:, None, :],
    )


def to_roots(plan, encs, distances):
    received = [encs[0]]
    roots = [
        (row, root)
        for row in range(plan.rows)
        for root in range(plan.rows)
        if abs(row - root) in distances
    ]
    for slot in range(1, len(encs)):
        if slot == 1 or 1 in distances:
            source = lambda root: root ^ slot
        else:
            source = lambda root: (root ^ 2) // 2 * 2 + slot - 2
        pairs = [(row * plan.rows + source(root), row * plan.rows + root) for row, root in roots]
        received.append(lax.ppermute(encs[slot], ("row", "col"), pairs))
    return received


def on_device_line(
    rows, amplitudes, integrals, virtual_energy, occupied_energy, virtual_count, occupied_count
):
    n = rows
    plan = Plan(
        amplitudes.shape, integrals.shape, rows, virtual_energy.shape[0], occupied_energy.shape[0]
    )
    swap = [(i, i ^ 1) for i in range(n)]
    sibling = lambda x: lax.ppermute(x, "col", swap)
    sib_integrals = sibling(integrals)
    more, tab, pack_tab, dest, rel, *tables = line_tables(
        plan, virtual_energy, occupied_energy, virtual_count, occupied_count
    )
    packed = pack(plan, pack_tab, amplitudes, dest, rel)
    base_rows = plan.base_tiles * TILE_ROWS
    all_rows = plan.pay_tiles * TILE_ROWS
    pay = packed[:base_rows]

    def send_rest(packed):
        gathered = lax.all_gather(packed[base_rows:all_rows], "row")
        return jnp.stack([gathered, sibling(gathered)])

    def no_rest(packed):
        return jnp.zeros((2, n, all_rows - base_rows, LANES), BF16)

    rest = lax.cond(more > 0, send_rest, no_rest, packed)
    row = lax.axis_index("row")

    def work(kind, pays, encs):
        both = [x for pay in pays for x in (pay, sibling(pay))]
        return ladder_call(plan, kind, tab, rel, both, rest, integrals, sib_integrals, encs)

    right = lax.ppermute(pay, "row", [(i, i + 1) for i in range(n - 1)])
    left = lax.ppermute(pay, "row", [(i + 1, i) for i in range(n - 1)])
    encs = work((0, ""), [pay], [])
    sources = []
    for step in range(2, n):
        right, left, encs, tables = lax.optimization_barrier((right, left, encs, tables))
        if step < n - 1:
            ahead = (
                lax.ppermute(right, "row", [(i, i + 1) for i in range(step - 1, n - 1)]),
                lax.ppermute(left, "row", [(i + 1, i) for i in range(0, n - step)]),
            )
        else:
            last = jnp.where(row >= n // 2, right, left)
            last = lax.ppermute(last, "row", [(n - 2, n - 1), (1, 0)])
        if step == 2:
            encs = work((1, "right"), [right], encs)
            encs = work((1, "left"), [left], encs)
        else:
            sources += to_roots(plan, encs, (0, 1) if step == 3 else (step - 2,))
            encs = work((step - 1, ""), [right, left], [])
        if step < n - 1:
            right, left = ahead
    sources += to_roots(plan, encs, (n - 2,))
    last, sources = lax.optimization_barrier((last, sources))
    encs = work((n - 1, ""), [last], [])
    near_tab, encs = lax.optimization_barrier((tab, encs))
    far = to_roots(plan, encs, (n - 1,))
    update = finish(plan, tuple(range(n - 2)), near_tab, *tables, sources, [])
    return finish(plan, (n - 2,), tab, *tables, far, [update])


def solution(mesh):
    rows, cols = mesh.shape["row"], mesh.shape["col"]
    placed = (P(None, ("row", "occ"), "col"), P(None, "row", "col"), P(), P(), P(), P())
    on_device = on_device_general
    if rows == 4 and cols == 4:
        on_device = functools.partial(on_device_line, rows)
    return jax.shard_map(
        on_device,
        mesh=mesh,
        in_specs=placed,
        out_specs=P(None, ("col", "occ"), "row"),
        check_vma=False,
    )
```

```python
import functools
import jax
import jax.numpy as jnp
from jax import lax
from jax.experimental import pallas as pl
from jax.experimental.pallas import tpu as pltpu
from jax.sharding import PartitionSpec as P

F32, BF16, I32, I16 = jnp.float32, jnp.bfloat16, jnp.int32, jnp.int16
LANES = 128
TILE_ROWS = 16
ANY = pl.BlockSpec(memory_space=pl.ANY)


def table_value(values_table, positions):
    places = jnp.arange(values_table.shape[0], dtype=jnp.int32)
    matches = positions[..., None] == places
    return jnp.sum(jnp.where(matches, values_table, jnp.zeros((), values_table.dtype)), axis=-1)


def is_orbital(counts, orbital, capacity):
    return orbital % capacity < table_value(counts, orbital // capacity)


def pair_orbitals(slot, group_width, capacity, sym_count):
    symmetry = jnp.arange(sym_count, dtype=jnp.int32)[:, None]
    offset = slot // group_width
    first_orb = jnp.broadcast_to(slot % group_width, (sym_count, slot.shape[0]))
    second_orb = jnp.bitwise_xor(first_orb, symmetry * capacity + offset[None, :])
    mate = offset[None, :] * group_width + second_orb
    return (first_orb, second_orb, mate)


def mirror_block(block, row_index, col_index):
    return jnp.take(jnp.take(block, row_index, axis=0), col_index, axis=1)


def on_device_general(
    amplitudes, integrals, virtual_energy, occupied_energy, virtual_count, occupied_count
):
    row_number = lax.axis_index("row")
    col_number = lax.axis_index("col")
    occ_number = lax.axis_index("occ")
    sym_count = amplitudes.shape[0]
    share_rows = amplitudes.shape[1]
    tile_width = amplitudes.shape[2]
    virt_slots = virtual_energy.shape[0]
    occ_slots = occupied_energy.shape[0]
    virt_cap = virt_slots // 8
    occ_cap = occ_slots // 8
    gathered = lax.all_gather(amplitudes, "row", axis=1, tiled=True)
    gathered_row = jnp.arange(gathered.shape[1], dtype=jnp.int32)
    source_slot = (
        2 * (gathered_row // share_rows) + occ_number
    ) * share_rows + gathered_row % share_rows
    first_source, second_source, _ = pair_orbitals(source_slot, occ_slots, occ_cap, sym_count)
    source_ok = is_orbital(occupied_count, first_source, occ_cap) & is_orbital(
        occupied_count, second_source, occ_cap
    )
    contract_slot = col_number * tile_width + jnp.arange(tile_width, dtype=jnp.int32)
    first_contract, second_contract, _ = pair_orbitals(
        contract_slot, virt_slots, virt_cap, sym_count
    )
    contract_ok = is_orbital(virtual_count, first_contract, virt_cap) & is_orbital(
        virtual_count, second_contract, virt_cap
    )
    masked = jnp.where(
        source_ok[:, :, None] & contract_ok[:, None, :], gathered, jnp.zeros((), gathered.dtype)
    )
    summed = lax.psum_scatter(
        jnp.einsum("sqd,spd->qsp", masked, integrals, preferred_element_type=jnp.float32),
        "col",
        scatter_dimension=0,
        tiled=True,
    )
    ladder = summed.transpose(1, 0, 2)
    row_base = (2 * col_number + occ_number) * share_rows
    output_slot = row_base + jnp.arange(share_rows, dtype=jnp.int32)
    first_occupied, second_occupied, occupied_mate = pair_orbitals(
        output_slot, occ_slots, occ_cap, sym_count
    )
    col_base = row_number * tile_width
    output_pair = col_base + jnp.arange(tile_width, dtype=jnp.int32)
    first_virtual, second_virtual, virtual_mate = pair_orbitals(
        output_pair, virt_slots, virt_cap, sym_count
    )
    mirrored = jax.vmap(mirror_block)(ladder, occupied_mate - row_base, virtual_mate - col_base)
    symmetrized = ladder + mirrored
    hole_ok = is_orbital(occupied_count, first_occupied, occ_cap) & is_orbital(
        occupied_count, second_occupied, occ_cap
    )
    pair_ok = is_orbital(virtual_count, first_virtual, virt_cap) & is_orbital(
        virtual_count, second_virtual, virt_cap
    )
    pair_energy = table_value(virtual_energy, first_virtual) + table_value(
        virtual_energy, second_virtual
    )
    hole_energy = table_value(occupied_energy, first_occupied) + table_value(
        occupied_energy, second_occupied
    )
    denominator = pair_energy[:, None, :] - hole_energy[:, :, None]
    allowed = hole_ok[:, :, None] & pair_ok[:, None, :]
    return jnp.where(allowed, symmetrized / denominator, jnp.zeros((), jnp.float32))


class Plan:
    def __init__(self, amp_shape, int_shape, rows, virt_slots, occ_slots):
        self.syms, self.share, self.width = amp_shape
        self.pairs = int_shape[1]
        self.rows = rows
        self.virt_slots, self.occ_slots = virt_slots, occ_slots
        self.virt_cap, self.occ_cap = virt_slots // 8, occ_slots // 8
        self.tiles = self.width // LANES
        self.row_tiles = self.share // TILE_ROWS
        self.pay_tiles = self.syms * self.tiles * self.row_tiles
        self.pay_room = self.pay_tiles * TILE_ROWS + self.share
        self.enc_tiles = (self.share // 2 + self.occ_slots // 2) // TILE_ROWS
        self.at_ndt = 2
        self.at_first = self.at_ndt + 2 * self.syms
        self.at_reps = self.at_first + 2 * self.syms * self.tiles
        self.at_self = self.at_reps + self.syms * rows
        self.at_more = self.at_self + self.syms * rows
        self.base_tiles = self.pay_tiles * 43 // 64
        enc_rows = self.enc_tiles * TILE_ROWS
        self.enc_shapes = [(enc_rows, self.pairs + LANES)] * (rows - 1) + [
            (self.share // 2, self.pairs + LANES)
        ]


def row_counts(plan, tab, sym, share):
    reps = tab[plan.at_reps + sym * plan.rows + share]
    selfs = tab[plan.at_self + sym * plan.rows + share]
    return reps, selfs, padded(2 * reps + selfs)


def band(rel_row):
    return (lax.broadcasted_iota(I32, (2 * LANES, LANES), 0) == rel_row).astype(BF16)


def pack_kernel(plan, tab, amp, dest, rel, pay, acc):
    pay[...] = jnp.zeros_like(pay)
    base = jnp.int32(0)
    for sym in range(plan.syms):
        ndt, nrt = tab[sym], tab[plan.syms + sym]
        pick = (
            lax.broadcasted_iota(I32, (plan.share, plan.share), 0) == dest[sym : sym + 1, :]
        ).astype(BF16)
        compact = jnp.dot(pick, amp[sym], preferred_element_type=F32).astype(BF16)
        acc[...] = jnp.zeros_like(acc)
        for tile in range(plan.tiles):
            at = sym * plan.tiles + tile
            placed = lax.dot_general(
                compact[:, tile * LANES : (tile + 1) * LANES],
                band(rel[at : at + 1, :]),
                (((1,), (1,)), ((), ())),
                preferred_element_type=F32,
            )
            first = tab[2 * plan.syms + at]
            acc[first] += placed[:, :LANES]
            acc[first + 1] += placed[:, LANES:]

        def put(tile, _, base=base, nrt=nrt):
            start = pl.multiple_of((base + tile * nrt) * TILE_ROWS, TILE_ROWS)
            pay[pl.ds(start, plan.share), :] = acc[tile].astype(BF16)
            return 0

        lax.fori_loop(0, ndt, put, 0)
        base = base + nrt * ndt


def pack(plan, tab, amp, dest, rel):
    vm = pl.BlockSpec(memory_space=pltpu.VMEM)
    return pl.pallas_call(
        functools.partial(pack_kernel, plan),
        out_shape=jax.ShapeDtypeStruct((plan.pay_room, LANES), BF16),
        in_specs=[pl.BlockSpec(memory_space=pltpu.SMEM), vm, vm, vm],
        out_specs=vm,
        scratch_shapes=[pltpu.VMEM((plan.tiles + 1, plan.share, LANES), F32)],
        compiler_params=pltpu.CompilerParams(vmem_limit_bytes=40 << 20),
        name="pack",
    )(tab, amp, dest, rel)


def share_of(plan, row, kind):
    step, side = kind
    if step == 0:
        return row, row >= 0
    if side == "right":
        return row - step, row >= step
    if side == "left":
        return row + step, row + step < plan.rows
    share = jnp.where(row >= plan.rows // 2, row - step, row + step)
    return share, (share >= 0) & (share < plan.rows)


def lane_mates(plan, rows, sym, fbase, tile):
    flip = sym * plan.virt_cap + fbase + (tile * LANES) // plan.virt_slots
    return lax.broadcasted_iota(I32, (rows, LANES), 1) ^ flip


def lane_take(x, index):
    return jnp.take_along_axis(x, index, axis=1)


def ladder_kernel(plan, kind, count, pay_rows, tab, rel, *refs):
    pays, (rest, ints, sib_ints) = refs[:count], refs[count : count + 3]
    outs, (pay, held, dense, prod, enc, sems, int_sems) = refs[-7 - plan.rows : -7], refs[-7:]
    row, col = tab[0], tab[1]
    sym = lax.rem(col, 2)
    share, active = share_of(plan, row, kind)
    steps = held.shape[1]
    ptile = plan.pairs // steps

    def int_copies(pt):
        return [
            pltpu.make_async_copy(
                ref.at[sym, pl.ds(pt * ptile, ptile)], held.at[part, pt], int_sems.at[part, pt]
            )
            for part, ref in enumerate((ints, sib_ints))
        ]

    def pay_copies(pair):
        return [
            pltpu.make_async_copy(ref, pay.at[part, pl.ds(0, pay_rows)], sems.at[part])
            for part, ref in enumerate(pair)
        ]

    @pl.when(active)
    def _():
        for start in (pay_rows, plan.pay_room - plan.share):
            pay[:, start : start + plan.share, :] = jnp.zeros((2, plan.share, LANES), BF16)
        if count == 2:
            for copy in pay_copies(pays):
                copy.start()
        else:
            upper = row >= plan.rows // 2

            @pl.when(upper)
            def _():
                for copy in pay_copies(pays[:2]):
                    copy.start()

            @pl.when(jnp.logical_not(upper))
            def _():
                for copy in pay_copies(pays[2:]):
                    copy.start()

        for copy in pay_copies(pays[:2]):
            copy.wait()
        for pt in range(steps):
            for copy in int_copies(pt):
                copy.start()

        @pl.when(tab[plan.at_more] > 0)
        def _():
            for part in range(2):
                copy = pltpu.make_async_copy(
                    rest.at[part, share], pay.at[part, pl.ds(pay_rows, rest.shape[2])], sems.at[part]
                )
                copy.start()
                copy.wait()

        reps, selfs, nrt = row_counts(plan, tab, sym, share)
        _, _, nrt0 = row_counts(plan, tab, 0, share)
        rep_room = padded(reps) * TILE_ROWS
        lines = lax.broadcasted_iota(I32, (plan.share, plan.share), 1)
        spread = lines + jnp.where(lines < reps, 0, jnp.where(lines < 2 * reps, 1, 2)) * (
            rep_room - reps
        )
        spread = jnp.where(
            spread == lax.broadcasted_iota(I32, (plan.share, plan.share), 0), 1.0, 0.0
        ).astype(BF16)
        group = 4
        for part in range(2):
            ndt0 = tab[plan.at_ndt + part * plan.syms]
            ndt = tab[plan.at_ndt + part * plan.syms + sym]
            base = jnp.where(sym == 0, 0, nrt0 * ndt0)
            for at_tile in range(0, plan.tiles, group):
                filled = []
                for tile in range(at_tile, at_tile + group):
                    at = (part * plan.syms + sym) * plan.tiles + tile
                    first = tab[plan.at_first + at]
                    pieces = []
                    for step in range(2):
                        use = jnp.maximum(jnp.minimum(first + step, ndt - 1), 0)
                        start = pl.multiple_of((base + use * nrt) * TILE_ROWS, TILE_ROWS)
                        pieces.append(pay[part, pl.ds(start, plan.share), :])
                    filled.append(
                        jnp.dot(
                            jnp.concatenate(pieces, axis=1),
                            band(rel[pl.ds(at, 1), :]),
                            preferred_element_type=F32,
                        ).astype(BF16)
                    )
                dense[part, :, at_tile * LANES : (at_tile + group) * LANES] = jnp.dot(
                    spread, jnp.concatenate(filled, axis=1), preferred_element_type=F32
                ).astype(BF16)

        def multiply(pt, _):
            for copy in int_copies(pt):
                copy.wait()
            prod[:, pl.ds(pl.multiple_of(pt * ptile, ptile), ptile)] = lax.dot_general(
                dense[0], held[0, pt], (((1,), (1,)), ((), ())), preferred_element_type=F32
            ) + lax.dot_general(
                dense[1], held[1, pt], (((1,), (1,)), ((), ())), preferred_element_type=F32
            )
            return 0

        lax.fori_loop(0, steps, multiply, 0)

        fbase = row * (plan.pairs // plan.virt_slots)

        def chunk(k, _):
            to_row = pl.multiple_of(k * TILE_ROWS, TILE_ROWS)
            mate_row = pl.multiple_of(to_row + rep_room, TILE_ROWS)
            own_row = pl.multiple_of(jnp.where(to_row < rep_room, to_row, mate_row), TILE_ROWS)
            sums, top = [], None
            for v in range(plan.pairs // LANES):
                lanes = slice(v * LANES, (v + 1) * LANES)
                mirrored = lane_take(
                    prod[pl.ds(mate_row, TILE_ROWS), lanes],
                    lane_mates(plan, TILE_ROWS, sym, fbase, v),
                )
                both = prod[pl.ds(own_row, TILE_ROWS), lanes] + mirrored
                sums.append(both)
                top = jnp.abs(both) if top is None else jnp.maximum(top, jnp.abs(both))
            peak = jnp.maximum(jnp.max(top, axis=1, keepdims=True), 1e-30)
            power = jnp.floor(jnp.log2(32000.0 / peak))
            scale = jnp.exp2(power)
            for v, both in enumerate(sums):
                enc[pl.ds(to_row, TILE_ROWS), v * LANES : (v + 1) * LANES] = (
                    jnp.round(both * scale).astype(I32).astype(I16)
                )
            enc[pl.ds(to_row, TILE_ROWS), plan.pairs :] = (
                jnp.broadcast_to(power, (TILE_ROWS, LANES)).astype(I32).astype(I16)
            )
            return 0

        lax.fori_loop(0, padded(reps) + padded(selfs), chunk, 0)

        flip = col ^ share
        slot = jnp.where(flip < 2, flip, 2 + sym)
        for number, out in enumerate(outs):

            @pl.when(slot == number)
            def _(out=out):
                copy = pltpu.make_async_copy(enc.at[pl.ds(0, out.shape[0])], out, sems.at[0])
                copy.start()
                copy.wait()


def ladder_call(plan, kind, tab, rel, pays, rest, integrals, sib_integrals, encs):
    steps = 4
    n = plan.rows
    smem, vmem = (pl.BlockSpec(memory_space=space) for space in (pltpu.SMEM, pltpu.VMEM))
    first_enc = 5 + len(pays)
    return pl.pallas_call(
        functools.partial(ladder_kernel, plan, kind, len(pays), pays[0].shape[0]),
        out_shape=[jax.ShapeDtypeStruct(shape, I16) for shape in plan.enc_shapes],
        in_specs=[smem, vmem] + [ANY] * (len(pays) + 3 + len(encs)),
        out_specs=[ANY] * n,
        scratch_shapes=[
            pltpu.VMEM((2, plan.pay_room, LANES), BF16),
            pltpu.VMEM((2, steps, plan.pairs // steps, plan.width), BF16),
            pltpu.VMEM((2, plan.share, plan.width), BF16),
            pltpu.VMEM((plan.share, plan.pairs), F32),
            pltpu.VMEM(plan.enc_shapes[0], I16),
            pltpu.SemaphoreType.DMA((2,)),
            pltpu.SemaphoreType.DMA((2, steps)),
        ],
        input_output_aliases={first_enc + i: i for i in range(len(encs))},
        compiler_params=pltpu.CompilerParams(vmem_limit_bytes=34 << 20),
        cost_estimate=pl.CostEstimate(
            flops=2 * plan.syms * plan.share * plan.width * plan.pairs,
            bytes_accessed=2 * plan.syms * plan.width * plan.pairs,
            transcendentals=0,
        ),
        name="ladder",
    )(tab, rel, *pays, rest, integrals, sib_integrals, *encs)


def finish_kernel(plan, numbers, wtile, tab, line, hole, pair, pair_ok, *refs):
    n = plan.rows
    out, held, pick, whole, sems, out_sems = refs[-6:]
    row, col = tab[0], tab[1]
    core = lax.rem(col, 2)
    which = jnp.abs(row - col)
    steps = plan.pairs // wtile

    def fetch(sources):
        parts = [(core, 0), (1 - core, 0), (0, 1), (1, 1)]
        copies = [
            pltpu.make_async_copy(
                ref, held.at[sym, side, pl.ds(0, ref.shape[0])], sems.at[number]
            )
            for number, (ref, (sym, side)) in enumerate(zip(sources, parts))
        ]
        for copy in copies:
            copy.start()
        places = lax.broadcasted_iota(I32, pick.shape[2:], 1)
        for sym in range(plan.syms):
            for half in range(2):
                pick[sym, half] = (places + half * pick.shape[3] == line[sym, :, 0:1]).astype(BF16)
        for copy in copies:
            copy.wait()

    for place, number in enumerate(numbers):

        @pl.when(which == number)
        def _(sources=refs[n * place : n * (place + 1)]):
            fetch(sources)

    def put(step):
        lanes = pl.ds(pl.multiple_of(step * wtile, wtile), wtile)
        return pltpu.make_async_copy(whole.at[:, :, lanes], out.at[:, :, lanes], out_sems.at[step])

    def tile(step, _):
        fbase = row * (plan.pairs // plan.virt_slots) + step * (wtile // plan.virt_slots)
        for sym in range(plan.syms):
            count = plan.enc_shapes[0][0] if sym == 0 else plan.share // 2
            reps, selfs, _ = row_counts(plan, tab, sym, col)
            live = lax.broadcasted_iota(I32, (count, LANES), 0) < (
                padded(reps) + padded(selfs)
            ) * TILE_ROWS
            scales = [
                jnp.exp2(
                    -held[sym, side, pl.ds(0, count), pl.ds(plan.pairs, LANES)]
                    .astype(I32)
                    .astype(F32)
                )
                for side in range(2)
            ]
            spans = [
                pl.ds(pl.multiple_of(step * wtile + v * LANES, LANES), LANES)
                for v in range(wtile // LANES)
            ]
            terms = [[], []]
            for lanes in spans:
                left = jnp.where(
                    live,
                    held[sym, 0, pl.ds(0, count), lanes].astype(I32).astype(F32) * scales[0]
                    + held[sym, 1, pl.ds(0, count), lanes].astype(I32).astype(F32) * scales[1],
                    0.0,
                )
                for term in terms:
                    term.append(left.astype(BF16))
                    left = left - term[-1].astype(F32)
            terms = [jnp.concatenate(term, axis=1) for term in terms]
            halves = []
            for half in range(2):
                total = None
                for term in terms:
                    part = jnp.dot(pick[sym, half, :, :count], term, preferred_element_type=F32)
                    total = part if total is None else total + part
                halves.append(total)
            for v, lanes in enumerate(spans):
                cut = slice(v * LANES, (v + 1) * LANES)
                result = halves[0][:, cut] + lane_take(
                    halves[1][:, cut], lane_mates(plan, plan.share, sym, fbase, v)
                )
                allowed = (line[sym] >= 0) & (pair_ok[sym, :, lanes] > 0)
                whole[sym, :, lanes] = jnp.where(
                    allowed, result / (pair[sym, :, lanes] - hole[sym]), 0.0
                )
        put(step).start()
        return 0

    def drain(step, _):
        put(step).wait()
        return 0

    @pl.when((which >= numbers[0]) & (which <= numbers[-1]))
    def _():
        lax.fori_loop(0, steps, tile, 0)
        lax.fori_loop(0, steps, drain, 0)


def finish(plan, numbers, tab, line, hole, pair, pair_ok, sources, before):
    wtile = min(256, plan.pairs)
    smem, vmem = (pl.BlockSpec(memory_space=space) for space in (pltpu.SMEM, pltpu.VMEM))
    out = jax.ShapeDtypeStruct((plan.syms, plan.share, plan.pairs), F32)
    return pl.pallas_call(
        functools.partial(finish_kernel, plan, numbers, wtile),
        out_shape=out,
        in_specs=[smem] + [vmem] * 4 + [ANY] * (len(sources) + len(before)),
        out_specs=ANY,
        scratch_shapes=[
            pltpu.VMEM((plan.syms, 2) + plan.enc_shapes[0], I16),
            pltpu.VMEM((plan.syms, 2, plan.share, plan.enc_shapes[0][0]), BF16),
            pltpu.VMEM(out.shape, F32),
            pltpu.SemaphoreType.DMA((4,)),
            pltpu.SemaphoreType.DMA((plan.pairs // wtile,)),
        ],
        input_output_aliases={5 + len(sources): 0} if before else {},
        compiler_params=pltpu.CompilerParams(vmem_limit_bytes=30 << 20),
        name="finish",
    )(tab, line, hole, pair, pair_ok, *sources, *before)


def occupied_share(plan, counts, share_number):
    slot = share_number * plan.share + jnp.arange(plan.share, dtype=I32)
    first, second, mate = pair_orbitals(slot, plan.occ_slots, plan.occ_cap, plan.syms)
    ok = is_orbital(counts, first, plan.occ_cap) & is_orbital(counts, second, plan.occ_cap)
    lead = jnp.minimum(slot[None, :], mate)
    is_rep = ok & (first < second)
    is_self = ok & (first == second)
    before = slot[None, None, :] < lead[:, :, None]
    rank = jnp.sum((is_rep[:, None, :] & before).astype(I32), axis=-1)
    self_rank = jnp.sum((is_self[:, None, :] & before).astype(I32), axis=-1)
    return first, second, ok, is_rep, is_self, rank, self_rank


def padded(count):
    return (count + TILE_ROWS - 1) // TILE_ROWS


def line_tables(plan, virtual_energy, occupied_energy, virtual_count, occupied_count):
    row = lax.axis_index("row")
    col = lax.axis_index("col")
    occ = lax.axis_index("occ")
    syms = plan.syms
    slots = jnp.arange(2 * plan.rows * plan.share, dtype=I32)
    first, second, _ = pair_orbitals(slots, plan.occ_slots, plan.occ_cap, syms)
    ok = is_orbital(occupied_count, first, plan.occ_cap) & is_orbital(
        occupied_count, second, plan.occ_cap
    )
    grouped = lambda x: jnp.sum(x.astype(I32).reshape(syms, plan.rows, 2, plan.share), axis=-1)
    reps_all = grouped(ok & (first < second))
    selfs_all = grouped(ok & (first == second))
    reps = jnp.where(occ == 0, reps_all[:, :, 0], reps_all[:, :, 1])
    selfs = jnp.where(occ == 0, selfs_all[:, :, 0], selfs_all[:, :, 1])
    blocks = plan.rows
    slots = jnp.arange(blocks * plan.width, dtype=I32)
    first, second, _ = pair_orbitals(slots, plan.virt_slots, plan.virt_cap, syms)
    ok = is_orbital(virtual_count, first, plan.virt_cap) & is_orbital(
        virtual_count, second, plan.virt_cap
    )
    per_block = jnp.sum(ok.astype(I32).reshape(syms, blocks, plan.width), axis=-1)
    ndt_all = (per_block + LANES - 1) // LANES
    tiles_needed = jnp.max(
        jnp.sum(padded(2 * reps_all + selfs_all)[:, :, :, None] * ndt_all[:, None, None, :], axis=0)
    )
    more = (tiles_needed > plan.base_tiles).astype(I32)
    slot = (col ^ jnp.arange(2, dtype=I32))[:, None] * plan.width + jnp.arange(
        plan.width, dtype=I32
    )
    first, second, _ = pair_orbitals(slot.reshape(-1), plan.virt_slots, plan.virt_cap, syms)
    ok = is_orbital(virtual_count, first, plan.virt_cap) & is_orbital(
        virtual_count, second, plan.virt_cap
    )
    ok = jnp.swapaxes(ok.reshape(syms, 2, plan.tiles, LANES), 0, 1)
    per_tile = jnp.sum(ok.astype(I32), axis=-1)
    tile_ids = jnp.arange(plan.tiles, dtype=I32)
    starts = jnp.sum(
        jnp.where(tile_ids[None, :] < tile_ids[:, None], per_tile[:, :, None, :], 0), axis=-1
    )
    lane_ids = jnp.arange(LANES, dtype=I32)
    within = jnp.sum(
        (ok[..., None, :] & (lane_ids[None, :] < lane_ids[:, None])).astype(I32), axis=-1
    )
    firsts = starts // LANES
    rel = jnp.where(ok, within + (starts % LANES)[..., None], -1)
    ndt = (jnp.sum(per_tile, axis=-1) + LANES - 1) // LANES
    tab = jnp.concatenate(
        [
            jnp.stack([row, col]).astype(I32),
            ndt.reshape(-1),
            firsts.reshape(-1),
            reps.reshape(-1),
            selfs.reshape(-1),
            more[None],
        ]
    )
    _, _, ok, is_rep, is_self, rank, self_rank = occupied_share(
        plan, occupied_count, 2 * row + occ
    )
    n_rep = jnp.sum(is_rep.astype(I32), axis=-1, keepdims=True)
    dest = jnp.where(is_self, 2 * n_rep + self_rank, jnp.where(is_rep, rank, n_rep + rank))
    dest = jnp.where(ok, dest, -1)
    n_valid = jnp.sum(ok.astype(I32), axis=-1)
    pack_tab = jnp.concatenate([ndt[0], padded(n_valid), firsts[0].reshape(-1)])
    first, second, ok, is_rep, is_self, rank, self_rank = occupied_share(
        plan, occupied_count, 2 * col + occ
    )
    n_rep = jnp.sum(is_rep.astype(I32), axis=-1, keepdims=True)
    count = plan.enc_tiles * TILE_ROWS
    rep_room = padded(n_rep) * TILE_ROWS
    line = jnp.where(is_self, rep_room + self_rank, jnp.where(is_rep, rank, count + rank))
    line = jnp.where(ok, line, -1)
    hole = table_value(occupied_energy, first) + table_value(occupied_energy, second)
    slot = row * plan.pairs + jnp.arange(plan.pairs, dtype=I32)
    first, second, _ = pair_orbitals(slot, plan.virt_slots, plan.virt_cap, syms)
    pair_ok = is_orbital(virtual_count, first, plan.virt_cap) & is_orbital(
        virtual_count, second, plan.virt_cap
    )
    pair = table_value(virtual_energy, first) + table_value(virtual_energy, second)
    return (
        more,
        tab,
        pack_tab,
        dest,
        rel.reshape(2 * syms * plan.tiles, LANES),
        jnp.broadcast_to(line[:, :, None], line.shape + (LANES,)),
        jnp.broadcast_to(hole[:, :, None], hole.shape + (LANES,)),
        pair[:, None, :],
        pair_ok.astype(I32)[:, None, :],
    )


def to_roots(plan, encs, distance):
    received = [encs[0]]
    roots = [
        (row, root)
        for row in range(plan.rows)
        for root in range(plan.rows)
        if abs(row - root) == distance
    ]
    for slot in range(1, len(encs)):
        source = lambda root: root ^ 1 if slot == 1 else (root ^ 2) // 2 * 2 + slot - 2
        pairs = [(row * plan.rows + source(root), row * plan.rows + root) for row, root in roots]
        received.append(lax.ppermute(encs[slot], ("row", "col"), pairs))
    return received


def on_device_line(
    rows, amplitudes, integrals, virtual_energy, occupied_energy, virtual_count, occupied_count
):
    n = rows
    plan = Plan(
        amplitudes.shape, integrals.shape, rows, virtual_energy.shape[0], occupied_energy.shape[0]
    )
    swap = [(i, i ^ 1) for i in range(n)]
    sibling = lambda x: lax.ppermute(x, "col", swap)
    sib_integrals = sibling(integrals)
    more, tab, pack_tab, dest, rel, *tables = line_tables(
        plan, virtual_energy, occupied_energy, virtual_count, occupied_count
    )
    packed = pack(plan, pack_tab, amplitudes, dest, rel)
    base_rows = plan.base_tiles * TILE_ROWS
    all_rows = plan.pay_tiles * TILE_ROWS
    pay = packed[:base_rows]

    def send_rest(packed):
        gathered = lax.all_gather(packed[base_rows:all_rows], "row")
        return jnp.stack([gathered, sibling(gathered)])

    def no_rest(packed):
        return jnp.zeros((2, n, all_rows - base_rows, LANES), BF16)

    rest = lax.cond(more > 0, send_rest, no_rest, packed)
    row = lax.axis_index("row")

    def work(kind, pays, encs):
        both = [x for pay in pays for x in (pay, sibling(pay))]
        return ladder_call(plan, kind, tab, rel, both, rest, integrals, sib_integrals, encs)

    right = lax.ppermute(pay, "row", [(i, i + 1) for i in range(n - 1)])
    left = lax.ppermute(pay, "row", [(i + 1, i) for i in range(n - 1)])
    encs = work((0, ""), [pay], [])
    sources = []
    for step in range(2, n):
        right, left, encs, tables = lax.optimization_barrier((right, left, encs, tables))
        if step < n - 1:
            ahead = (
                lax.ppermute(right, "row", [(i, i + 1) for i in range(step - 1, n - 1)]),
                lax.ppermute(left, "row", [(i + 1, i) for i in range(0, n - step)]),
            )
        else:
            sums, last = lax.optimization_barrier((sums, jnp.where(row >= n // 2, right, left)))
            sources += sums
            last = lax.ppermute(last, "row", [(n - 2, n - 1), (1, 0)])
        sums = to_roots(plan, encs, step - 2)
        if step == 2:
            encs = work((1, "right"), [right], [])
            encs = work((1, "left"), [left], encs)
        else:
            encs = work((step - 1, ""), [right, left], [])
        if step < n - 1:
            right, left = ahead
    sources += sums + to_roots(plan, encs, n - 2)
    last, sources = lax.optimization_barrier((last, sources))
    encs = work((n - 1, ""), [last], [])
    near_tab, encs = lax.optimization_barrier((tab, encs))
    far = to_roots(plan, encs, n - 1)
    update = finish(plan, tuple(range(n - 1)), near_tab, *tables, sources, [])
    return finish(plan, (n - 1,), tab, *tables, far, [update])


def solution(mesh):
    rows, cols = mesh.shape["row"], mesh.shape["col"]
    placed = (P(None, ("row", "occ"), "col"), P(None, "row", "col"), P(), P(), P(), P())
    on_device = on_device_general
    if rows == 4 and cols == 4:
        on_device = functools.partial(on_device_line, rows)
    return jax.shard_map(
        on_device,
        mesh=mesh,
        in_specs=placed,
        out_specs=P(None, ("col", "occ"), "row"),
        check_vma=False,
    )
```

```python
import functools
import jax
import jax.numpy as jnp
from jax import lax
from jax.experimental import pallas as pl
from jax.experimental.pallas import tpu as pltpu
from jax.sharding import PartitionSpec as P

F32, BF16, I32, I16 = jnp.float32, jnp.bfloat16, jnp.int32, jnp.int16
LANES = 128
TILE_ROWS = 16
ANY = pl.BlockSpec(memory_space=pl.ANY)


def table_value(values_table, positions):
    places = jnp.arange(values_table.shape[0], dtype=jnp.int32)
    matches = positions[..., None] == places
    return jnp.sum(jnp.where(matches, values_table, jnp.zeros((), values_table.dtype)), axis=-1)


def is_orbital(counts, orbital, capacity):
    return orbital % capacity < table_value(counts, orbital // capacity)


def pair_orbitals(slot, group_width, capacity, sym_count):
    symmetry = jnp.arange(sym_count, dtype=jnp.int32)[:, None]
    offset = slot // group_width
    first_orb = jnp.broadcast_to(slot % group_width, (sym_count, slot.shape[0]))
    second_orb = jnp.bitwise_xor(first_orb, symmetry * capacity + offset[None, :])
    mate = offset[None, :] * group_width + second_orb
    return (first_orb, second_orb, mate)


def mirror_block(block, row_index, col_index):
    return jnp.take(jnp.take(block, row_index, axis=0), col_index, axis=1)


def on_device_general(
    amplitudes, integrals, virtual_energy, occupied_energy, virtual_count, occupied_count
):
    row_number = lax.axis_index("row")
    col_number = lax.axis_index("col")
    occ_number = lax.axis_index("occ")
    sym_count = amplitudes.shape[0]
    share_rows = amplitudes.shape[1]
    tile_width = amplitudes.shape[2]
    virt_slots = virtual_energy.shape[0]
    occ_slots = occupied_energy.shape[0]
    virt_cap = virt_slots // 8
    occ_cap = occ_slots // 8
    gathered = lax.all_gather(amplitudes, "row", axis=1, tiled=True)
    gathered_row = jnp.arange(gathered.shape[1], dtype=jnp.int32)
    source_slot = (
        2 * (gathered_row // share_rows) + occ_number
    ) * share_rows + gathered_row % share_rows
    first_source, second_source, _ = pair_orbitals(source_slot, occ_slots, occ_cap, sym_count)
    source_ok = is_orbital(occupied_count, first_source, occ_cap) & is_orbital(
        occupied_count, second_source, occ_cap
    )
    contract_slot = col_number * tile_width + jnp.arange(tile_width, dtype=jnp.int32)
    first_contract, second_contract, _ = pair_orbitals(
        contract_slot, virt_slots, virt_cap, sym_count
    )
    contract_ok = is_orbital(virtual_count, first_contract, virt_cap) & is_orbital(
        virtual_count, second_contract, virt_cap
    )
    masked = jnp.where(
        source_ok[:, :, None] & contract_ok[:, None, :], gathered, jnp.zeros((), gathered.dtype)
    )
    summed = lax.psum_scatter(
        jnp.einsum("sqd,spd->qsp", masked, integrals, preferred_element_type=jnp.float32),
        "col",
        scatter_dimension=0,
        tiled=True,
    )
    ladder = summed.transpose(1, 0, 2)
    row_base = (2 * col_number + occ_number) * share_rows
    output_slot = row_base + jnp.arange(share_rows, dtype=jnp.int32)
    first_occupied, second_occupied, occupied_mate = pair_orbitals(
        output_slot, occ_slots, occ_cap, sym_count
    )
    col_base = row_number * tile_width
    output_pair = col_base + jnp.arange(tile_width, dtype=jnp.int32)
    first_virtual, second_virtual, virtual_mate = pair_orbitals(
        output_pair, virt_slots, virt_cap, sym_count
    )
    mirrored = jax.vmap(mirror_block)(ladder, occupied_mate - row_base, virtual_mate - col_base)
    symmetrized = ladder + mirrored
    hole_ok = is_orbital(occupied_count, first_occupied, occ_cap) & is_orbital(
        occupied_count, second_occupied, occ_cap
    )
    pair_ok = is_orbital(virtual_count, first_virtual, virt_cap) & is_orbital(
        virtual_count, second_virtual, virt_cap
    )
    pair_energy = table_value(virtual_energy, first_virtual) + table_value(
        virtual_energy, second_virtual
    )
    hole_energy = table_value(occupied_energy, first_occupied) + table_value(
        occupied_energy, second_occupied
    )
    denominator = pair_energy[:, None, :] - hole_energy[:, :, None]
    allowed = hole_ok[:, :, None] & pair_ok[:, None, :]
    return jnp.where(allowed, symmetrized / denominator, jnp.zeros((), jnp.float32))


class Plan:
    def __init__(self, amp_shape, int_shape, rows, virt_slots, occ_slots):
        self.syms, self.share, self.width = amp_shape
        self.pairs = int_shape[1]
        self.rows = rows
        self.virt_slots, self.occ_slots = virt_slots, occ_slots
        self.virt_cap, self.occ_cap = virt_slots // 8, occ_slots // 8
        self.tiles = self.width // LANES
        self.row_tiles = self.share // TILE_ROWS
        self.pay_tiles = self.syms * self.tiles * self.row_tiles
        self.pay_room = self.pay_tiles * TILE_ROWS + self.share
        self.enc_tiles = (self.share // 2 + self.occ_slots // 2) // TILE_ROWS
        self.at_ndt = 2
        self.at_first = self.at_ndt + 2 * self.syms
        self.at_reps = self.at_first + 2 * self.syms * self.tiles
        self.at_self = self.at_reps + self.syms * rows
        self.at_more = self.at_self + self.syms * rows
        self.base_tiles = self.pay_tiles * 43 // 64
        enc_rows = self.enc_tiles * TILE_ROWS
        self.enc_shapes = [(enc_rows, self.pairs + LANES)] * (rows - 1) + [
            (self.share // 2, self.pairs + LANES)
        ]


def row_counts(plan, tab, sym, share):
    reps = tab[plan.at_reps + sym * plan.rows + share]
    selfs = tab[plan.at_self + sym * plan.rows + share]
    return reps, selfs, padded(2 * reps + selfs)


def band(rel_row):
    return (lax.broadcasted_iota(I32, (2 * LANES, LANES), 0) == rel_row).astype(BF16)


def pack_kernel(plan, tab, amp, dest, rel, pay, acc):
    pay[...] = jnp.zeros_like(pay)
    base = jnp.int32(0)
    for sym in range(plan.syms):
        ndt, nrt = tab[sym], tab[plan.syms + sym]
        pick = (
            lax.broadcasted_iota(I32, (plan.share, plan.share), 0) == dest[sym : sym + 1, :]
        ).astype(BF16)
        compact = jnp.dot(pick, amp[sym], preferred_element_type=F32).astype(BF16)
        acc[...] = jnp.zeros_like(acc)
        for tile in range(plan.tiles):
            at = sym * plan.tiles + tile
            placed = lax.dot_general(
                compact[:, tile * LANES : (tile + 1) * LANES],
                band(rel[at : at + 1, :]),
                (((1,), (1,)), ((), ())),
                preferred_element_type=F32,
            )
            first = tab[2 * plan.syms + at]
            acc[first] += placed[:, :LANES]
            acc[first + 1] += placed[:, LANES:]

        def put(tile, _, base=base, nrt=nrt):
            start = pl.multiple_of((base + tile * nrt) * TILE_ROWS, TILE_ROWS)
            pay[pl.ds(start, plan.share), :] = acc[tile].astype(BF16)
            return 0

        lax.fori_loop(0, ndt, put, 0)
        base = base + nrt * ndt


def pack(plan, tab, amp, dest, rel):
    vm = pl.BlockSpec(memory_space=pltpu.VMEM)
    return pl.pallas_call(
        functools.partial(pack_kernel, plan),
        out_shape=jax.ShapeDtypeStruct((plan.pay_room, LANES), BF16),
        in_specs=[pl.BlockSpec(memory_space=pltpu.SMEM), vm, vm, vm],
        out_specs=vm,
        scratch_shapes=[pltpu.VMEM((plan.tiles + 1, plan.share, LANES), F32)],
        compiler_params=pltpu.CompilerParams(vmem_limit_bytes=40 << 20),
        name="pack",
    )(tab, amp, dest, rel)


def share_of(plan, row, kind):
    step, side = kind
    if step == 0:
        return row, row >= 0
    if side == "right":
        return row - step, row >= step
    if side == "left":
        return row + step, row + step < plan.rows
    share = jnp.where(row >= plan.rows // 2, row - step, row + step)
    return share, (share >= 0) & (share < plan.rows)


def lane_mates(plan, rows, sym, fbase, tile):
    flip = sym * plan.virt_cap + fbase + (tile * LANES) // plan.virt_slots
    return lax.broadcasted_iota(I32, (rows, LANES), 1) ^ flip


def lane_take(x, index):
    return jnp.take_along_axis(x, index, axis=1)


def ladder_kernel(plan, kind, count, pay_rows, tab, rel, *refs):
    pays, (rest, ints, sib_ints) = refs[:count], refs[count : count + 3]
    outs, (pay, held, dense, prod, enc, sems, int_sems) = refs[-7 - plan.rows : -7], refs[-7:]
    row, col = tab[0], tab[1]
    sym = lax.rem(col, 2)
    share, active = share_of(plan, row, kind)
    steps = held.shape[1]
    ptile = plan.pairs // steps

    def int_copies(pt):
        return [
            pltpu.make_async_copy(
                ref.at[sym, pl.ds(pt * ptile, ptile)], held.at[part, pt], int_sems.at[part, pt]
            )
            for part, ref in enumerate((ints, sib_ints))
        ]

    def pay_copies(pair):
        return [
            pltpu.make_async_copy(ref, pay.at[part, pl.ds(0, pay_rows)], sems.at[part])
            for part, ref in enumerate(pair)
        ]

    @pl.when(active)
    def _():
        for start in (pay_rows, plan.pay_room - plan.share):
            pay[:, start : start + plan.share, :] = jnp.zeros((2, plan.share, LANES), BF16)
        if count == 2:
            for copy in pay_copies(pays):
                copy.start()
        else:
            upper = row >= plan.rows // 2

            @pl.when(upper)
            def _():
                for copy in pay_copies(pays[:2]):
                    copy.start()

            @pl.when(jnp.logical_not(upper))
            def _():
                for copy in pay_copies(pays[2:]):
                    copy.start()

        for copy in int_copies(0):
            copy.start()
        for copy in pay_copies(pays[:2]):
            copy.wait()
        for pt in range(1, steps):
            for copy in int_copies(pt):
                copy.start()

        @pl.when(tab[plan.at_more] > 0)
        def _():
            for part in range(2):
                copy = pltpu.make_async_copy(
                    rest.at[part, share], pay.at[part, pl.ds(pay_rows, rest.shape[2])], sems.at[part]
                )
                copy.start()
                copy.wait()

        reps, selfs, nrt = row_counts(plan, tab, sym, share)
        _, _, nrt0 = row_counts(plan, tab, 0, share)
        rep_room = padded(reps) * TILE_ROWS
        lines = lax.broadcasted_iota(I32, (plan.share, plan.share), 1)
        spread = lines + jnp.where(lines < reps, 0, jnp.where(lines < 2 * reps, 1, 2)) * (
            rep_room - reps
        )
        spread = jnp.where(
            spread == lax.broadcasted_iota(I32, (plan.share, plan.share), 0), 1.0, 0.0
        ).astype(BF16)
        group = 4
        for part in range(2):
            ndt0 = tab[plan.at_ndt + part * plan.syms]
            ndt = tab[plan.at_ndt + part * plan.syms + sym]
            base = jnp.where(sym == 0, 0, nrt0 * ndt0)
            for at_tile in range(0, plan.tiles, group):
                filled = []
                for tile in range(at_tile, at_tile + group):
                    at = (part * plan.syms + sym) * plan.tiles + tile
                    first = tab[plan.at_first + at]
                    pieces = []
                    for step in range(2):
                        use = jnp.maximum(jnp.minimum(first + step, ndt - 1), 0)
                        start = pl.multiple_of((base + use * nrt) * TILE_ROWS, TILE_ROWS)
                        pieces.append(pay[part, pl.ds(start, plan.share), :])
                    filled.append(
                        jnp.dot(
                            jnp.concatenate(pieces, axis=1),
                            band(rel[pl.ds(at, 1), :]),
                            preferred_element_type=F32,
                        ).astype(BF16)
                    )
                dense[part, :, at_tile * LANES : (at_tile + group) * LANES] = jnp.dot(
                    spread, jnp.concatenate(filled, axis=1), preferred_element_type=F32
                ).astype(BF16)

        def multiply(pt, _):
            for copy in int_copies(pt):
                copy.wait()
            prod[:, pl.ds(pl.multiple_of(pt * ptile, ptile), ptile)] = lax.dot_general(
                dense[0], held[0, pt], (((1,), (1,)), ((), ())), preferred_element_type=F32
            ) + lax.dot_general(
                dense[1], held[1, pt], (((1,), (1,)), ((), ())), preferred_element_type=F32
            )
            return 0

        lax.fori_loop(0, steps, multiply, 0)

        fbase = row * (plan.pairs // plan.virt_slots)

        def chunk(k, _):
            to_row = pl.multiple_of(k * TILE_ROWS, TILE_ROWS)
            mate_row = pl.multiple_of(to_row + rep_room, TILE_ROWS)
            own_row = pl.multiple_of(jnp.where(to_row < rep_room, to_row, mate_row), TILE_ROWS)
            sums, top = [], None
            for v in range(plan.pairs // LANES):
                lanes = slice(v * LANES, (v + 1) * LANES)
                mirrored = lane_take(
                    prod[pl.ds(mate_row, TILE_ROWS), lanes],
                    lane_mates(plan, TILE_ROWS, sym, fbase, v),
                )
                both = prod[pl.ds(own_row, TILE_ROWS), lanes] + mirrored
                sums.append(both)
                top = jnp.abs(both) if top is None else jnp.maximum(top, jnp.abs(both))
            peak = jnp.maximum(jnp.max(top, axis=1, keepdims=True), 1e-30)
            power = jnp.floor(jnp.log2(32000.0 / peak))
            scale = jnp.exp2(power)
            for v, both in enumerate(sums):
                enc[pl.ds(to_row, TILE_ROWS), v * LANES : (v + 1) * LANES] = (
                    jnp.round(both * scale).astype(I32).astype(I16)
                )
            enc[pl.ds(to_row, TILE_ROWS), plan.pairs :] = (
                jnp.broadcast_to(power, (TILE_ROWS, LANES)).astype(I32).astype(I16)
            )
            return 0

        lax.fori_loop(0, padded(reps) + padded(selfs), chunk, 0)

        flip = col ^ share
        slot = jnp.where(flip < 2, flip, 2 + sym)
        for number, out in enumerate(outs):

            @pl.when(slot == number)
            def _(out=out):
                copy = pltpu.make_async_copy(enc.at[pl.ds(0, out.shape[0])], out, sems.at[0])
                copy.start()
                copy.wait()


def ladder_call(plan, kind, tab, rel, pays, rest, integrals, sib_integrals, encs):
    steps = 4
    n = plan.rows
    smem, vmem = (pl.BlockSpec(memory_space=space) for space in (pltpu.SMEM, pltpu.VMEM))
    first_enc = 5 + len(pays)
    return pl.pallas_call(
        functools.partial(ladder_kernel, plan, kind, len(pays), pays[0].shape[0]),
        out_shape=[jax.ShapeDtypeStruct(shape, I16) for shape in plan.enc_shapes],
        in_specs=[smem, vmem] + [ANY] * (len(pays) + 3 + len(encs)),
        out_specs=[ANY] * n,
        scratch_shapes=[
            pltpu.VMEM((2, plan.pay_room, LANES), BF16),
            pltpu.VMEM((2, steps, plan.pairs // steps, plan.width), BF16),
            pltpu.VMEM((2, plan.share, plan.width), BF16),
            pltpu.VMEM((plan.share, plan.pairs), F32),
            pltpu.VMEM(plan.enc_shapes[0], I16),
            pltpu.SemaphoreType.DMA((2,)),
            pltpu.SemaphoreType.DMA((2, steps)),
        ],
        input_output_aliases={first_enc + i: i for i in range(len(encs))},
        compiler_params=pltpu.CompilerParams(vmem_limit_bytes=34 << 20),
        cost_estimate=pl.CostEstimate(
            flops=2 * plan.syms * plan.share * plan.width * plan.pairs,
            bytes_accessed=2 * plan.syms * plan.width * plan.pairs,
            transcendentals=0,
        ),
        name="ladder",
    )(tab, rel, *pays, rest, integrals, sib_integrals, *encs)


def finish_kernel(plan, numbers, wtile, tab, line, hole, pair, pair_ok, *refs):
    n = plan.rows
    out, held, pick, whole, sems, out_sems = refs[-6:]
    row, col = tab[0], tab[1]
    core = lax.rem(col, 2)
    which = jnp.abs(row - col)
    steps = plan.pairs // wtile

    def fetch(sources):
        parts = [(core, 0), (1 - core, 0), (0, 1), (1, 1)]
        copies = [
            pltpu.make_async_copy(
                ref, held.at[sym, side, pl.ds(0, ref.shape[0])], sems.at[number]
            )
            for number, (ref, (sym, side)) in enumerate(zip(sources, parts))
        ]
        for copy in copies:
            copy.start()
        places = lax.broadcasted_iota(I32, pick.shape[2:], 1)
        for sym in range(plan.syms):
            for half in range(2):
                pick[sym, half] = (places + half * pick.shape[3] == line[sym, :, 0:1]).astype(BF16)
        for copy in copies:
            copy.wait()

    for place, number in enumerate(numbers):

        @pl.when(which == number)
        def _(sources=refs[n * place : n * (place + 1)]):
            fetch(sources)

    def put(step):
        lanes = pl.ds(pl.multiple_of(step * wtile, wtile), wtile)
        return pltpu.make_async_copy(whole.at[:, :, lanes], out.at[:, :, lanes], out_sems.at[step])

    def tile(step, _):
        fbase = row * (plan.pairs // plan.virt_slots) + step * (wtile // plan.virt_slots)
        for sym in range(plan.syms):
            count = plan.enc_shapes[0][0] if sym == 0 else plan.share // 2
            reps, selfs, _ = row_counts(plan, tab, sym, col)
            live = lax.broadcasted_iota(I32, (count, LANES), 0) < (
                padded(reps) + padded(selfs)
            ) * TILE_ROWS
            scales = [
                jnp.exp2(
                    -held[sym, side, pl.ds(0, count), pl.ds(plan.pairs, LANES)]
                    .astype(I32)
                    .astype(F32)
                )
                for side in range(2)
            ]
            spans = [
                pl.ds(pl.multiple_of(step * wtile + v * LANES, LANES), LANES)
                for v in range(wtile // LANES)
            ]
            terms = [[], []]
            for lanes in spans:
                left = jnp.where(
                    live,
                    held[sym, 0, pl.ds(0, count), lanes].astype(I32).astype(F32) * scales[0]
                    + held[sym, 1, pl.ds(0, count), lanes].astype(I32).astype(F32) * scales[1],
                    0.0,
                )
                for term in terms:
                    term.append(left.astype(BF16))
                    left = left - term[-1].astype(F32)
            terms = [jnp.concatenate(term, axis=1) for term in terms]
            halves = []
            for half in range(2):
                total = None
                for term in terms:
                    part = jnp.dot(pick[sym, half, :, :count], term, preferred_element_type=F32)
                    total = part if total is None else total + part
                halves.append(total)
            for v, lanes in enumerate(spans):
                cut = slice(v * LANES, (v + 1) * LANES)
                result = halves[0][:, cut] + lane_take(
                    halves[1][:, cut], lane_mates(plan, plan.share, sym, fbase, v)
                )
                allowed = (line[sym] >= 0) & (pair_ok[sym, :, lanes] > 0)
                whole[sym, :, lanes] = jnp.where(
                    allowed, result / (pair[sym, :, lanes] - hole[sym]), 0.0
                )
        put(step).start()
        return 0

    def drain(step, _):
        put(step).wait()
        return 0

    @pl.when((which >= numbers[0]) & (which <= numbers[-1]))
    def _():
        lax.fori_loop(0, steps, tile, 0)
        lax.fori_loop(0, steps, drain, 0)


def finish(plan, numbers, tab, line, hole, pair, pair_ok, sources, before):
    wtile = min(512, plan.pairs)
    smem, vmem = (pl.BlockSpec(memory_space=space) for space in (pltpu.SMEM, pltpu.VMEM))
    out = jax.ShapeDtypeStruct((plan.syms, plan.share, plan.pairs), F32)
    return pl.pallas_call(
        functools.partial(finish_kernel, plan, numbers, wtile),
        out_shape=out,
        in_specs=[smem] + [vmem] * 4 + [ANY] * (len(sources) + len(before)),
        out_specs=ANY,
        scratch_shapes=[
            pltpu.VMEM((plan.syms, 2) + plan.enc_shapes[0], I16),
            pltpu.VMEM((plan.syms, 2, plan.share, plan.enc_shapes[0][0]), BF16),
            pltpu.VMEM(out.shape, F32),
            pltpu.SemaphoreType.DMA((4,)),
            pltpu.SemaphoreType.DMA((plan.pairs // wtile,)),
        ],
        input_output_aliases={5 + len(sources): 0} if before else {},
        compiler_params=pltpu.CompilerParams(vmem_limit_bytes=30 << 20),
        name="finish",
    )(tab, line, hole, pair, pair_ok, *sources, *before)


def occupied_share(plan, counts, share_number):
    slot = share_number * plan.share + jnp.arange(plan.share, dtype=I32)
    first, second, mate = pair_orbitals(slot, plan.occ_slots, plan.occ_cap, plan.syms)
    ok = is_orbital(counts, first, plan.occ_cap) & is_orbital(counts, second, plan.occ_cap)
    lead = jnp.minimum(slot[None, :], mate)
    is_rep = ok & (first < second)
    is_self = ok & (first == second)
    before = slot[None, None, :] < lead[:, :, None]
    rank = jnp.sum((is_rep[:, None, :] & before).astype(I32), axis=-1)
    self_rank = jnp.sum((is_self[:, None, :] & before).astype(I32), axis=-1)
    return first, second, ok, is_rep, is_self, rank, self_rank


def padded(count):
    return (count + TILE_ROWS - 1) // TILE_ROWS


def line_tables(plan, virtual_energy, occupied_energy, virtual_count, occupied_count):
    row = lax.axis_index("row")
    col = lax.axis_index("col")
    occ = lax.axis_index("occ")
    syms = plan.syms
    slots = jnp.arange(2 * plan.rows * plan.share, dtype=I32)
    first, second, _ = pair_orbitals(slots, plan.occ_slots, plan.occ_cap, syms)
    ok = is_orbital(occupied_count, first, plan.occ_cap) & is_orbital(
        occupied_count, second, plan.occ_cap
    )
    grouped = lambda x: jnp.sum(x.astype(I32).reshape(syms, plan.rows, 2, plan.share), axis=-1)
    reps_all = grouped(ok & (first < second))
    selfs_all = grouped(ok & (first == second))
    reps = jnp.where(occ == 0, reps_all[:, :, 0], reps_all[:, :, 1])
    selfs = jnp.where(occ == 0, selfs_all[:, :, 0], selfs_all[:, :, 1])
    blocks = plan.rows
    slots = jnp.arange(blocks * plan.width, dtype=I32)
    first, second, _ = pair_orbitals(slots, plan.virt_slots, plan.virt_cap, syms)
    ok = is_orbital(virtual_count, first, plan.virt_cap) & is_orbital(
        virtual_count, second, plan.virt_cap
    )
    per_block = jnp.sum(ok.astype(I32).reshape(syms, blocks, plan.width), axis=-1)
    ndt_all = (per_block + LANES - 1) // LANES
    tiles_needed = jnp.max(
        jnp.sum(padded(2 * reps_all + selfs_all)[:, :, :, None] * ndt_all[:, None, None, :], axis=0)
    )
    more = (tiles_needed > plan.base_tiles).astype(I32)
    slot = (col ^ jnp.arange(2, dtype=I32))[:, None] * plan.width + jnp.arange(
        plan.width, dtype=I32
    )
    first, second, _ = pair_orbitals(slot.reshape(-1), plan.virt_slots, plan.virt_cap, syms)
    ok = is_orbital(virtual_count, first, plan.virt_cap) & is_orbital(
        virtual_count, second, plan.virt_cap
    )
    ok = jnp.swapaxes(ok.reshape(syms, 2, plan.tiles, LANES), 0, 1)
    per_tile = jnp.sum(ok.astype(I32), axis=-1)
    tile_ids = jnp.arange(plan.tiles, dtype=I32)
    starts = jnp.sum(
        jnp.where(tile_ids[None, :] < tile_ids[:, None], per_tile[:, :, None, :], 0), axis=-1
    )
    lane_ids = jnp.arange(LANES, dtype=I32)
    within = jnp.sum(
        (ok[..., None, :] & (lane_ids[None, :] < lane_ids[:, None])).astype(I32), axis=-1
    )
    firsts = starts // LANES
    rel = jnp.where(ok, within + (starts % LANES)[..., None], -1)
    ndt = (jnp.sum(per_tile, axis=-1) + LANES - 1) // LANES
    tab = jnp.concatenate(
        [
            jnp.stack([row, col]).astype(I32),
            ndt.reshape(-1),
            firsts.reshape(-1),
            reps.reshape(-1),
            selfs.reshape(-1),
            more[None],
        ]
    )
    _, _, ok, is_rep, is_self, rank, self_rank = occupied_share(
        plan, occupied_count, 2 * row + occ
    )
    n_rep = jnp.sum(is_rep.astype(I32), axis=-1, keepdims=True)
    dest = jnp.where(is_self, 2 * n_rep + self_rank, jnp.where(is_rep, rank, n_rep + rank))
    dest = jnp.where(ok, dest, -1)
    n_valid = jnp.sum(ok.astype(I32), axis=-1)
    pack_tab = jnp.concatenate([ndt[0], padded(n_valid), firsts[0].reshape(-1)])
    first, second, ok, is_rep, is_self, rank, self_rank = occupied_share(
        plan, occupied_count, 2 * col + occ
    )
    n_rep = jnp.sum(is_rep.astype(I32), axis=-1, keepdims=True)
    count = plan.enc_tiles * TILE_ROWS
    rep_room = padded(n_rep) * TILE_ROWS
    line = jnp.where(is_self, rep_room + self_rank, jnp.where(is_rep, rank, count + rank))
    line = jnp.where(ok, line, -1)
    hole = table_value(occupied_energy, first) + table_value(occupied_energy, second)
    slot = row * plan.pairs + jnp.arange(plan.pairs, dtype=I32)
    first, second, _ = pair_orbitals(slot, plan.virt_slots, plan.virt_cap, syms)
    pair_ok = is_orbital(virtual_count, first, plan.virt_cap) & is_orbital(
        virtual_count, second, plan.virt_cap
    )
    pair = table_value(virtual_energy, first) + table_value(virtual_energy, second)
    return (
        more,
        tab,
        pack_tab,
        dest,
        rel.reshape(2 * syms * plan.tiles, LANES),
        jnp.broadcast_to(line[:, :, None], line.shape + (LANES,)),
        jnp.broadcast_to(hole[:, :, None], hole.shape + (LANES,)),
        pair[:, None, :],
        pair_ok.astype(I32)[:, None, :],
    )


def to_roots(plan, encs, distance):
    received = [encs[0]]
    roots = [
        (row, root)
        for row in range(plan.rows)
        for root in range(plan.rows)
        if abs(row - root) == distance
    ]
    for slot in range(1, len(encs)):
        source = lambda root: root ^ 1 if slot == 1 else (root ^ 2) // 2 * 2 + slot - 2
        pairs = [(row * plan.rows + source(root), row * plan.rows + root) for row, root in roots]
        received.append(lax.ppermute(encs[slot], ("row", "col"), pairs))
    return received


def on_device_line(
    rows, amplitudes, integrals, virtual_energy, occupied_energy, virtual_count, occupied_count
):
    n = rows
    plan = Plan(
        amplitudes.shape, integrals.shape, rows, virtual_energy.shape[0], occupied_energy.shape[0]
    )
    swap = [(i, i ^ 1) for i in range(n)]
    sibling = lambda x: lax.ppermute(x, "col", swap)
    sib_integrals = sibling(integrals)
    more, tab, pack_tab, dest, rel, *tables = line_tables(
        plan, virtual_energy, occupied_energy, virtual_count, occupied_count
    )
    packed = pack(plan, pack_tab, amplitudes, dest, rel)
    base_rows = plan.base_tiles * TILE_ROWS
    all_rows = plan.pay_tiles * TILE_ROWS
    pay = packed[:base_rows]

    def send_rest(packed):
        gathered = lax.all_gather(packed[base_rows:all_rows], "row")
        return jnp.stack([gathered, sibling(gathered)])

    def no_rest(packed):
        return jnp.zeros((2, n, all_rows - base_rows, LANES), BF16)

    rest = lax.cond(more > 0, send_rest, no_rest, packed)
    row = lax.axis_index("row")

    def work(kind, pays, encs):
        both = [x for pay in pays for x in (pay, sibling(pay))]
        return ladder_call(plan, kind, tab, rel, both, rest, integrals, sib_integrals, encs)

    right = lax.ppermute(pay, "row", [(i, i + 1) for i in range(n - 1)])
    left = lax.ppermute(pay, "row", [(i + 1, i) for i in range(n - 1)])
    encs = work((0, ""), [pay], [])
    sources = []
    for step in range(2, n):
        right, left, encs, tables = lax.optimization_barrier((right, left, encs, tables))
        if step < n - 1:
            ahead = (
                lax.ppermute(right, "row", [(i, i + 1) for i in range(step - 1, n - 1)]),
                lax.ppermute(left, "row", [(i + 1, i) for i in range(0, n - step)]),
            )
        else:
            sums, last = lax.optimization_barrier((sums, jnp.where(row >= n // 2, right, left)))
            sources += sums
            last = lax.ppermute(last, "row", [(n - 2, n - 1), (1, 0)])
        sums = to_roots(plan, encs, step - 2)
        if step == 2:
            encs = work((1, "right"), [right], [])
            encs = work((1, "left"), [left], encs)
        else:
            encs = work((step - 1, ""), [right, left], [])
        if step < n - 1:
            right, left = ahead
    sources += sums + to_roots(plan, encs, n - 2)
    last, sources = lax.optimization_barrier((last, sources))
    encs = work((n - 1, ""), [last], [])
    near_tab, encs = lax.optimization_barrier((tab, encs))
    far = to_roots(plan, encs, n - 1)
    update = finish(plan, tuple(range(n - 1)), near_tab, *tables, sources, [])
    return finish(plan, (n - 1,), tab, *tables, far, [update])


def solution(mesh):
    rows, cols = mesh.shape["row"], mesh.shape["col"]
    placed = (P(None, ("row", "occ"), "col"), P(None, "row", "col"), P(), P(), P(), P())
    on_device = on_device_general
    if rows == 4 and cols == 4:
        on_device = functools.partial(on_device_line, rows)
    return jax.shard_map(
        on_device,
        mesh=mesh,
        in_specs=placed,
        out_specs=P(None, ("col", "occ"), "row"),
        check_vma=False,
    )
```
